128 devices in a mesh: row: 8 (over x, core), col: 16 (over y, z).
Axes of the slice: x: 4, y: 4, z: 4, core: 2. Of those that a mesh axis runs over, the one named last changes fastest.
Arguments:
- front_block: bfloat16 [16384, 16384], P('row', 'col'), may hold values from -0.046875 to 0.046875
- probe_right: bfloat16 [16384, 256], P('col'), may hold values from -6 to 6
- probe_left: bfloat16 [16384, 256], P('row'), may hold values from -6 to 6
- row_leaf: int32 [16384, 1], replicated, may hold values from 0 to 127; in each aligned block of 128 rows (0 to 127, 128 to 255, ...) at most 2 rows name the same one
- tree_leaf: int32 [128], replicated, may hold values from 0 to 127, each once
Outputs:
- coupling: float32 [128, 256, 256], P(('row', 'col'))
- merged: float32 [128, 256, 256], P(('row', 'col'))
The draws below stay inside these ranges and needn't reach their ends.
Inputs may be any that keep to these rules, and one draw needn't show every extreme that they name: `row_leaf`: in each aligned block of 128 rows no leaf is named by more than 2 rows, a bound that some block reaches; every leaf has one row or more. `tree_leaf`: each leaf once. Positions that differ in bit 0 are siblings; their parents, at positions differing in bit 1, are siblings at the next level.
All inputs are finite; a program needn't handle non-finite values.
Results may differ from the reference program's by a relative error of at most 0.0092.
Values may be sent and summed in bfloat16 or wider, within the bound.
A program may use at most 64 MiB of HBM per device.

```python
import math
import jax
import jax.numpy as jnp
import numpy as np
from jax import lax

NA = 16384
SAMPLES = 256
ROWS_DEV = 128
CAP = 2
WIDEST = 256
DEVICES = 128


def block_scale(own_key, extent, cuts, low, top_value):
    loudness = 1.0
    for position, shards_of in cuts:
        heights = jax.random.uniform(jax.random.fold_in(jax.random.fold_in(own_key, 6), position), (shards_of,), jnp.float32, low / len(cuts), top_value / len(cuts))
        loudness = loudness * jnp.repeat(jnp.exp(heights), extent[position] // shards_of).reshape((-1,) + (1,) * (len(extent) - 1 - position))
    return loudness


def routed_block(stream_key, own, number, rows, count, top, reach, slope):
    sequence = jax.random.permutation(stream_key, count)
    heavy_load, usual = shares(count, rows * top, reach, slope, True), shares(count, rows * top, reach, slope, False)
    places = jnp.arange(count)

    def named(tallies, turn):
        used = int((tallies > 0).sum())
        fixed = max(1, used // 4)
        shifted = fixed + (places - fixed + turn * (used - fixed)) % max(1, count - fixed)
        return jnp.zeros((count,), jnp.int32).at[sequence[jnp.where(places < fixed, places, shifted)]].set(jnp.asarray(tallies, jnp.int32))

    tallies = jnp.where(number % 4 == 0, named(heavy_load, number // 4), named(usual, number - number // 4 - 1))
    mixed = jax.random.permutation(jax.random.fold_in(own, 3), count)
    donor, sink = mixed[0:count // 2 * 2:2], mixed[1:count // 2 * 2:2]
    slack = jnp.minimum(tallies[donor] - 1, reach - tallies[sink]) // 2
    slack = jnp.where((donor == sequence[0]) | (sink == sequence[0]) | (tallies[sink] == 0), 0, jnp.maximum(slack, 0))
    shifted = jax.random.randint(jax.random.fold_in(own, 4), (count // 2,), 0, 1 << 20) % (slack + 1)
    tallies = tallies.at[donor].add(-shifted).at[sink].add(shifted)
    items = jnp.searchsorted(jnp.cumsum(tallies), jnp.arange(rows * top), side="right").astype(jnp.int32)
    table = items.reshape(top, rows).T
    table = table[jax.random.permutation(jax.random.fold_in(own, 1), rows)]
    turn = jax.random.randint(jax.random.fold_in(own, 2), (rows, 1), 0, top)
    return jnp.take_along_axis(table, (jnp.arange(top)[None, :] + turn) % top, axis=1)


def shares(amount, total, bound, lean, full):
    portions = [(1 << 20) // math.isqrt(rank ** lean) + 1 for rank in range(1, amount + 1)]
    largest = bound if full else min(bound, max(-(-total // amount), total * portions[0] // sum(portions)))
    least = 1 if total - largest >= amount - 1 else 0
    given, spare = [largest] + [least] * (amount - 1), total - largest - least * (amount - 1)
    while spare > 0:
        candidates = [i for i in range(1, amount) if given[i] < largest] or [i for i in range(1, amount) if given[i] < bound]
        mass, left = sum([portions[i] for i in candidates]), spare
        for i in candidates:
            more = min(bound - given[i], max(1, left * portions[i] // mass), spare)
            given[i] = given[i] + more
            spare = spare - more
    return np.array(given)


def bell_draw(rng, dims, scale, limit, split=(), held_as=jnp.bfloat16):
    gain = block_scale(rng, dims, split, -0.22, 0.18) if split else 1.0
    values = jax.random.normal(rng, dims, jnp.float32) * scale * gain
    return jnp.minimum(jnp.maximum(values, -limit), limit).astype(held_as)


def setup_inputs(seed: int = 0) -> dict:
    key_of = jax.random.split(jax.random.key(seed), 6)
    front_block = bell_draw(key_of[0], (NA, NA), NA ** -0.5, 0.046875, ((0, 8), (1, 16)))
    probe_right = bell_draw(key_of[1], (NA, SAMPLES), 1.0, 6.0, ((0, 16),))
    probe_left = bell_draw(key_of[2], (NA, SAMPLES), 1.0, 6.0, ((0, 8),))
    row_leaf_keys = jax.random.split(jax.random.fold_in(key_of[3], 1), NA // ROWS_DEV)
    row_leaf_turns = jax.random.permutation(jax.random.fold_in(key_of[3], 3), NA // ROWS_DEV)
    row_leaf = jax.vmap(lambda own, number: routed_block(jax.random.fold_in(key_of[3], 2), own, number, ROWS_DEV, DEVICES, 1, CAP, 2))(row_leaf_keys, row_leaf_turns).reshape((NA, 1))
    tree_leaf = jax.random.permutation(key_of[4], DEVICES).astype(jnp.int32)
    return dict(front_block=front_block, probe_right=probe_right, probe_left=probe_left, row_leaf=row_leaf, tree_leaf=tree_leaf)


eps = 1e-05

def exact_dot(left, right):
    return jnp.dot(left.astype(jnp.float32), right.astype(jnp.float32), precision=lax.Precision.HIGHEST, preferred_element_type=jnp.float32)

def whiten_cross(gram_sum, squares, cross_sum):
    width = gram_sum.shape[0]
    ridge = squares / width + eps
    factor = jnp.linalg.cholesky(gram_sum + ridge * jnp.eye(width, dtype=jnp.float32))
    return lax.linalg.triangular_solve(factor, cross_sum, left_side=True, lower=True)

def merge_pair(mine, other):
    gram_sum = exact_dot(mine.T, mine) + exact_dot(other.T, other)
    squares = jnp.sum(mine * mine) + jnp.sum(other * other)
    cross_sum = exact_dot(mine.T, other) + exact_dot(other.T, mine)
    return whiten_cross(gram_sum, squares, cross_sum)

def reference(front_block, probe_right, probe_left, row_leaf, tree_leaf):
    leaves = row_leaf[:, 0]
    height = min(NA, 1024)
    contract = (((0,), (0,)), ((), ()))

    def row_step(carry, start):
        back_full, back_diag = carry
        front_rows = lax.dynamic_slice_in_dim(front_block, start, height, 0)
        here = lax.dynamic_slice_in_dim(leaves, start, height, 0)
        masked = jnp.where(here[:, None] == leaves[None, :], front_rows, jnp.zeros_like(front_rows))
        left_rows = lax.dynamic_slice_in_dim(probe_left, start, height, 0)
        forward_full = jnp.dot(front_rows.astype(jnp.float32), probe_right.astype(jnp.float32), preferred_element_type=jnp.float32)
        forward_diag = jnp.dot(masked.astype(jnp.float32), probe_right.astype(jnp.float32), preferred_element_type=jnp.float32)
        back_full = back_full + lax.dot_general(front_rows.astype(jnp.float32), left_rows.astype(jnp.float32), contract, preferred_element_type=jnp.float32)
        back_diag = back_diag + lax.dot_general(masked.astype(jnp.float32), left_rows.astype(jnp.float32), contract, preferred_element_type=jnp.float32)
        return ((back_full, back_diag), (forward_full - forward_diag).astype(jnp.bfloat16))
    zeros_back = jnp.zeros((NA, SAMPLES), jnp.float32)
    starts_rows = jnp.arange(NA // height, dtype=jnp.int32) * height
    (back_full, back_diag), forward_rows = lax.scan(row_step, (zeros_back, zeros_back), starts_rows)
    sample_rows = forward_rows.reshape(NA, SAMPLES)
    sample_back = (back_full - back_diag).astype(jnp.bfloat16)
    positions = jnp.arange(DEVICES, dtype=jnp.int32)
    counts = jnp.sum((leaves[:, None] == positions[None, :]).astype(jnp.int32), axis=0)
    starts = (jnp.cumsum(counts) - counts).astype(jnp.int32)
    sorted_rows = jnp.argsort(leaves, stable=True).astype(jnp.int32)
    padded = jnp.concatenate([sorted_rows, jnp.zeros((WIDEST,), jnp.int32)])
    slot_ids = jnp.arange(WIDEST, dtype=jnp.int32)

    def per_leaf(leaf):
        row_ids = lax.dynamic_slice_in_dim(padded, starts[leaf], WIDEST)
        is_valid = slot_ids < counts[leaf]
        s_rows = jnp.where(is_valid[:, None], sample_rows[row_ids], jnp.zeros((), jnp.bfloat16))
        t_rows = jnp.where(is_valid[:, None], sample_back[row_ids], jnp.zeros((), jnp.bfloat16))
        gram_sum = jnp.dot(s_rows.T.astype(jnp.float32), s_rows.astype(jnp.float32), preferred_element_type=jnp.float32)
        cross_sum = jnp.dot(s_rows.T.astype(jnp.float32), t_rows.astype(jnp.float32), preferred_element_type=jnp.float32)
        wide_rows = s_rows.astype(jnp.float32)
        squares = jnp.sum(wide_rows * wide_rows)
        return whiten_cross(gram_sum, squares, cross_sum)
    coupling = lax.map(per_leaf, tree_leaf)
    merged = coupling
    for depth_level in range(2):
        partner = merged[jnp.bitwise_xor(positions, 1 << depth_level)]
        merged = jax.vmap(merge_pair)(merged, partner)
    return (coupling, merged)
```

```python
import functools

import jax
import jax.numpy as jnp
from jax import lax
from jax.experimental import pallas as pl
from jax.experimental.pallas import tpu as pltpu
from jax.sharding import PartitionSpec as P

eps = 1e-05
F32, BF16 = jnp.float32, jnp.bfloat16
AB = (((1,), (0,)), ((), ()))
ABT = (((1,), (1,)), ((), ()))
ATB = (((0,), (0,)), ((), ()))


def split(value):
    high = value.astype(BF16)
    return high, (value - high.astype(F32)).astype(BF16)


def mm(left, right, dims=AB):
    return lax.dot_general(left, right, dims, preferred_element_type=F32)


def mm3(left, right, dims=AB):
    return mm(left[0], right[0], dims) + (mm(left[0], right[1], dims) + mm(left[1], right[0], dims))


def whiten(gram, squares, cross, out_ref, b_ref, x_ref, g_ref):
    width = gram.shape[0]
    row = lax.broadcasted_iota(jnp.int32, (width, width), 0)
    col = lax.broadcasted_iota(jnp.int32, (width, width), 1)
    below, diag = row > col, row == col

    def half(value):
        return jnp.where(below, value, jnp.where(diag, 0.5 * value, 0.0))

    def factor(value):
        return jnp.where(below, -value, jnp.where(diag, 1.5 - 0.5 * value, 0.0)).astype(BF16)

    ridge = squares / width + eps
    inv_root = lax.rsqrt(ridge)
    unit = gram * (inv_root * inv_root) + diag.astype(F32)
    g_high, g_low = split(unit)
    g_ref[0] = g_high
    g_ref[1] = g_low
    rhs = split(cross * inv_root)
    square = mm(g_high, g_high)
    fourth = jnp.sum(jnp.sum(square * square, axis=1, keepdims=True), axis=0, keepdims=True)
    scale = 0.99 * lax.rsqrt(jnp.sqrt(fourth))
    fourth_scalar = jnp.sum(fourth)
    steps = jnp.int32(3)
    for k in range(1, 8):
        steps = steps + (fourth_scalar > 2.25 ** (4 * k)).astype(jnp.int32)
    extra = (fourth_scalar > 48.0**4).astype(jnp.int32)

    b0 = unit * scale
    t0 = factor(b0)
    b_ref[...] = mm(mm(t0, b0.astype(BF16)).astype(BF16), t0, ABT)
    x_ref[...] = t0.astype(F32) * jnp.sqrt(scale)

    def step(_, carry):
        b = b_ref[...]
        t = factor(b)
        y = mm(t, b.astype(BF16))
        x = mm(t, x_ref[...].astype(BF16))
        b_ref[...] = mm(y.astype(BF16), t, ABT)
        x_ref[...] = x
        return carry

    lax.fori_loop(1, steps, step, 0)

    def error(x):
        y = split(mm3(x, (g_ref[0], g_ref[1])))
        return half(mm3(y, x, ABT) - diag.astype(F32))

    def fix(_, carry):
        x = split(x_ref[...])
        x_ref[...] = x_ref[...] - mm3(split(error(x)), x)
        return carry

    lax.fori_loop(0, extra, fix, 0)
    x = split(x_ref[...])
    z = mm3(x, rhs)
    out_ref[...] = z - mm(error(x).astype(BF16), z.astype(BF16))


def total(value):
    return jnp.sum(jnp.sum(value, axis=1, keepdims=True), axis=0, keepdims=True)


def leaf_kernel(s_ref, u_ref, out_ref, b_ref, x_ref, g_ref):
    s, u = s_ref[...], u_ref[...]
    wide = s.astype(F32)
    whiten(mm(s, s, ATB), total(wide * wide), mm(s, u, ATB), out_ref, b_ref, x_ref, g_ref)


def merge_kernel(p_ref, q_ref, out_ref, b_ref, x_ref, g_ref):
    p, q = p_ref[...], q_ref[...]
    squares = total(p * p + q * q)
    ps, qs = split(p), split(q)
    gram = mm3(ps, ps, ATB) + mm3(qs, qs, ATB)
    cross = mm3(ps, qs, ATB) + mm3(qs, ps, ATB)
    whiten(gram, squares, cross, out_ref, b_ref, x_ref, g_ref)


def dense_call(kernel, left, right):
    width = left.shape[1]
    whole = pl.BlockSpec(memory_space=pltpu.VMEM)
    return pl.pallas_call(
        kernel,
        out_shape=jax.ShapeDtypeStruct((width, width), F32),
        in_specs=[whole, whole],
        out_specs=whole,
        scratch_shapes=[
            pltpu.VMEM((width, width), F32),
            pltpu.VMEM((width, width), F32),
            pltpu.VMEM((2, width, width), BF16),
        ],
    )(left, right)


def from_partner(value, axis, distance):
    mask = 2**distance
    pairs = [(source, source ^ mask) for source in range(lax.axis_size(axis))]
    return lax.ppermute(value, axis, pairs)


def spread(rows, block_leaf, places, capacity, devices):
    count = rows.shape[0]
    positions = jnp.arange(devices, dtype=jnp.int32)
    owner = jnp.sum(jnp.where(block_leaf[:, None] == positions[None, :], places[None, :], 0), axis=1)
    order = jnp.arange(count, dtype=jnp.int32)
    earlier = (owner[:, None] == owner[None, :]) & (order[None, :] < order[:, None])
    slot = owner * capacity + jnp.sum(earlier.astype(jnp.int32), axis=1)
    chosen = (jnp.arange(devices * capacity, dtype=jnp.int32)[:, None] == slot[None, :]).astype(BF16)
    return jnp.dot(chosen, rows, preferred_element_type=F32).astype(BF16)


def per_device(front_block, probe_right, probe_left, row_leaf, tree_leaf):
    row_count = lax.axis_size("row")
    col_count = lax.axis_size("col")
    devices = row_count * col_count
    row_index = lax.axis_index("row")
    col_index = lax.axis_index("col")
    tile_rows, tile_cols = front_block.shape
    samples = probe_right.shape[1]
    leaves = row_leaf[:, 0]
    rows_dev = leaves.shape[0] // devices
    capacity = 2
    rows_leaf = lax.dynamic_slice_in_dim(leaves, row_index * tile_rows, tile_rows)
    cols_leaf = lax.dynamic_slice_in_dim(leaves, col_index * tile_cols, tile_cols)
    same_leaf = rows_leaf[:, None] == cols_leaf[None, :]
    off = jnp.where(same_leaf, jnp.zeros_like(front_block), front_block)
    forward = jnp.dot(off, probe_right, preferred_element_type=F32).astype(BF16)
    backward = lax.dot_general(off, probe_left, ATB, preferred_element_type=F32)
    forward = lax.all_to_all(forward.reshape(col_count, rows_dev, samples), "col", 0, 0, tiled=True)
    backward = lax.all_to_all(backward.reshape(row_count, rows_dev, samples), "row", 0, 0, tiled=True)
    sample_rows = jnp.sum(forward.astype(F32), axis=0).astype(BF16)
    sample_back = jnp.sum(backward, axis=0).astype(BF16)
    positions = jnp.arange(devices, dtype=jnp.int32)
    places = jnp.sum(jnp.where(tree_leaf[:, None] == positions[None, :], positions[:, None], 0), axis=0)

    def block_leaf(block):
        return lax.dynamic_slice_in_dim(leaves, block * rows_dev, rows_dev)

    forward_send = spread(sample_rows, block_leaf(row_index * col_count + col_index), places, capacity, devices)
    backward_send = spread(sample_back, block_leaf(col_index * row_count + row_index), places, capacity, devices)
    both = jnp.stack(
        [forward_send.reshape(devices, capacity, samples), backward_send.reshape(devices, capacity, samples)], axis=1
    )
    both = lax.all_to_all(both, ("row", "col"), split_axis=0, concat_axis=0, tiled=True)
    forward_recv = both[:, 0].reshape(devices * capacity, samples)
    backward_recv = both[:, 1].reshape(row_count, col_count, capacity, samples)
    backward_recv = backward_recv.transpose(1, 0, 2, 3).reshape(devices * capacity, samples)
    coupling = dense_call(leaf_kernel, forward_recv, backward_recv)
    merged = coupling
    for level in range(2):
        merged = dense_call(merge_kernel, merged, from_partner(merged, "col", level))
    return (coupling[None], merged[None])


def solution(mesh):
    return jax.shard_map(
        per_device,
        mesh=mesh,
        in_specs=(P("row", "col"), P("col", None), P("row", None), P(), P()),
        out_specs=(P(("row", "col"), None, None), P(("row", "col"), None, None)),
        check_vma=False,
    )
```

```python
import functools

import jax
import jax.numpy as jnp
from jax import lax
from jax.experimental import pallas as pl
from jax.experimental.pallas import tpu as pltpu
from jax.sharding import PartitionSpec as P

eps = 1e-05
F32, BF16 = jnp.float32, jnp.bfloat16
AB = (((1,), (0,)), ((), ()))
ABT = (((1,), (1,)), ((), ()))
ATB = (((0,), (0,)), ((), ()))


def split(value):
    high = value.astype(BF16)
    return high, (value - high.astype(F32)).astype(BF16)


def mm(left, right, dims=AB):
    return lax.dot_general(left, right, dims, preferred_element_type=F32)


def mm3(left, right, dims=AB):
    return mm(left[0], right[0], dims) + (mm(left[0], right[1], dims) + mm(left[1], right[0], dims))


def whiten(gram, squares, cross, out_ref, send_ref, b_ref, x_ref, g_ref):
    width = gram.shape[0]
    row = lax.broadcasted_iota(jnp.int32, (width, width), 0)
    col = lax.broadcasted_iota(jnp.int32, (width, width), 1)
    below, diag = row > col, row == col

    def half(value):
        return jnp.where(below, value, jnp.where(diag, 0.5 * value, 0.0))

    def factor(value):
        return jnp.where(below, -value, jnp.where(diag, 1.5 - 0.5 * value, 0.0)).astype(BF16)

    ridge = squares / width + eps
    inv_root = lax.rsqrt(ridge)
    unit = gram * (inv_root * inv_root) + diag.astype(F32)
    g_high, g_low = split(unit)
    g_ref[0] = g_high
    g_ref[1] = g_low
    rhs = split(cross * inv_root)
    square = mm(g_high, g_high)
    fourth = jnp.sum(jnp.sum(square * square, axis=1, keepdims=True), axis=0, keepdims=True)
    scale = 0.99 * lax.rsqrt(jnp.sqrt(fourth))
    fourth_scalar = jnp.sum(fourth)
    steps = jnp.int32(3)
    for k in range(1, 8):
        steps = steps + (fourth_scalar > 2.25 ** (4 * k)).astype(jnp.int32)
    extra = (fourth_scalar > 48.0**4).astype(jnp.int32)

    b0 = unit * scale
    t0 = factor(b0)
    b_ref[...] = mm(mm(t0, b0.astype(BF16)).astype(BF16), t0, ABT)
    x_ref[...] = t0.astype(F32) * jnp.sqrt(scale)

    def step(_, carry):
        b = b_ref[...]
        t = factor(b)
        y = mm(t, b.astype(BF16))
        x = mm(t, x_ref[...].astype(BF16))
        b_ref[...] = mm(y.astype(BF16), t, ABT)
        x_ref[...] = x
        return carry

    lax.fori_loop(1, steps, step, 0)

    def error(x):
        y = split(mm3(x, (g_ref[0], g_ref[1])))
        return half(mm3(y, x, ABT) - diag.astype(F32))

    def fix(_, carry):
        x = split(x_ref[...])
        x_ref[...] = x_ref[...] - mm3(split(error(x)), x)
        return carry

    lax.fori_loop(0, extra, fix, 0)
    x = split(x_ref[...])
    z = mm3(x, rhs)
    out = z - mm(error(x).astype(BF16), z.astype(BF16))
    out_ref[...] = out
    send_ref[...] = out.astype(BF16)


def total(value):
    return jnp.sum(jnp.sum(value, axis=1, keepdims=True), axis=0, keepdims=True)


def leaf_kernel(s_ref, u_ref, out_ref, *refs):
    s, u = s_ref[...], u_ref[...]
    wide = s.astype(F32)
    whiten(mm(s, s, ATB), total(wide * wide), mm(s, u, ATB), out_ref, *refs)


def merge_kernel(p_ref, q_ref, out_ref, *refs):
    p, q = p_ref[...], q_ref[...]
    wide = q.astype(F32)
    squares = total(p * p + wide * wide)
    high, low = split(p)
    gram = mm3((high, low), (high, low), ATB) + mm(q, q, ATB)
    cross = mm(high, q, ATB) + mm(low, q, ATB)
    whiten(gram, squares, cross + cross.T, out_ref, *refs)


def dense_call(kernel, left, right):
    width = left.shape[1]
    whole = pl.BlockSpec(memory_space=pltpu.VMEM)
    return pl.pallas_call(
        kernel,
        out_shape=(jax.ShapeDtypeStruct((width, width), F32), jax.ShapeDtypeStruct((width, width), BF16)),
        in_specs=[whole, whole],
        out_specs=(whole, whole),
        scratch_shapes=[
            pltpu.VMEM((width, width), F32),
            pltpu.VMEM((width, width), F32),
            pltpu.VMEM((2, width, width), BF16),
        ],
    )(left, right)


def from_partner(value, axis, distance):
    mask = 2**distance
    pairs = [(source, source ^ mask) for source in range(lax.axis_size(axis))]
    return lax.ppermute(value, axis, pairs)


def spread(rows, block_leaf, places, capacity, devices):
    count = rows.shape[0]
    positions = jnp.arange(devices, dtype=jnp.int32)
    owner = jnp.sum(jnp.where(block_leaf[:, None] == positions[None, :], places[None, :], 0), axis=1)
    order = jnp.arange(count, dtype=jnp.int32)
    earlier = (owner[:, None] == owner[None, :]) & (order[None, :] < order[:, None])
    slot = owner * capacity + jnp.sum(earlier.astype(jnp.int32), axis=1)
    chosen = (jnp.arange(devices * capacity, dtype=jnp.int32)[:, None] == slot[None, :]).astype(BF16)
    return jnp.dot(chosen, rows, preferred_element_type=F32).astype(BF16)


def per_device(front_block, probe_right, probe_left, row_leaf, tree_leaf):
    row_count = lax.axis_size("row")
    col_count = lax.axis_size("col")
    devices = row_count * col_count
    row_index = lax.axis_index("row")
    col_index = lax.axis_index("col")
    tile_rows, tile_cols = front_block.shape
    samples = probe_right.shape[1]
    leaves = row_leaf[:, 0]
    rows_dev = leaves.shape[0] // devices
    capacity = 2
    rows_leaf = lax.dynamic_slice_in_dim(leaves, row_index * tile_rows, tile_rows)
    cols_leaf = lax.dynamic_slice_in_dim(leaves, col_index * tile_cols, tile_cols)
    same_leaf = rows_leaf[:, None] == cols_leaf[None, :]
    off = jnp.where(same_leaf, jnp.zeros_like(front_block), front_block)
    forward = jnp.dot(off, probe_right, preferred_element_type=F32).astype(BF16)
    backward = lax.dot_general(off, probe_left, ATB, preferred_element_type=F32)
    forward = lax.all_to_all(forward.reshape(col_count, rows_dev, samples), "col", 0, 0, tiled=True)
    backward = lax.all_to_all(backward.reshape(row_count, rows_dev, samples), "row", 0, 0, tiled=True)
    sample_rows = jnp.sum(forward.astype(F32), axis=0).astype(BF16)
    sample_back = jnp.sum(backward, axis=0).astype(BF16)
    positions = jnp.arange(devices, dtype=jnp.int32)
    places = jnp.sum(jnp.where(tree_leaf[:, None] == positions[None, :], positions[:, None], 0), axis=0)

    def block_leaf(block):
        return lax.dynamic_slice_in_dim(leaves, block * rows_dev, rows_dev)

    forward_send = spread(sample_rows, block_leaf(row_index * col_count + col_index), places, capacity, devices)
    backward_send = spread(sample_back, block_leaf(col_index * row_count + row_index), places, capacity, devices)
    both = jnp.stack(
        [forward_send.reshape(devices, capacity, samples), backward_send.reshape(devices, capacity, samples)], axis=1
    )
    both = lax.all_to_all(both, ("row", "col"), split_axis=0, concat_axis=0, tiled=True)
    forward_recv = both[:, 0].reshape(devices * capacity, samples)
    backward_recv = both[:, 1].reshape(row_count, col_count, capacity, samples)
    backward_recv = backward_recv.transpose(1, 0, 2, 3).reshape(devices * capacity, samples)
    coupling, sent = dense_call(leaf_kernel, forward_recv, backward_recv)
    merged = coupling
    for level in range(2):
        merged, sent = dense_call(merge_kernel, merged, from_partner(sent, "col", level))
    return (coupling[None], merged[None])


def solution(mesh):
    return jax.shard_map(
        per_device,
        mesh=mesh,
        in_specs=(P("row", "col"), P("col", None), P("row", None), P(), P()),
        out_specs=(P(("row", "col"), None, None), P(("row", "col"), None, None)),
        check_vma=False,
    )
```

```python
import functools

import jax
import jax.numpy as jnp
from jax import lax
from jax.experimental import pallas as pl
from jax.experimental.pallas import tpu as pltpu
from jax.sharding import PartitionSpec as P

eps = 1e-05
F32, BF16 = jnp.float32, jnp.bfloat16
AB = (((1,), (0,)), ((), ()))
ABT = (((1,), (1,)), ((), ()))
ATB = (((0,), (0,)), ((), ()))


def split(value):
    high = value.astype(BF16)
    return high, (value - high.astype(F32)).astype(BF16)


def mm(left, right, dims=AB):
    return lax.dot_general(left, right, dims, preferred_element_type=F32)


def mm3(left, right, dims=AB):
    return mm(left[0], right[0], dims) + (mm(left[0], right[1], dims) + mm(left[1], right[0], dims))


def whiten(gram, squares, cross, out_ref, send_ref, b_ref, x_ref, g_ref):
    width = gram.shape[0]
    row = lax.broadcasted_iota(jnp.int32, (width, width), 0)
    col = lax.broadcasted_iota(jnp.int32, (width, width), 1)
    below, diag = row > col, row == col

    def half(value):
        return jnp.where(below, value, jnp.where(diag, 0.5 * value, 0.0))

    def factor(value):
        return jnp.where(below, -value, jnp.where(diag, 1.5 - 0.5 * value, 0.0)).astype(BF16)

    ridge = squares / width + eps
    inv_root = lax.rsqrt(ridge)
    unit = gram * (inv_root * inv_root) + diag.astype(F32)
    g_high, g_low = split(unit)
    g_ref[0] = g_high
    g_ref[1] = g_low
    rhs = split(cross * inv_root)
    square = mm(g_high, g_high)
    fourth = jnp.sum(jnp.sum(square * square, axis=1, keepdims=True), axis=0, keepdims=True)
    scale = 0.99 * lax.rsqrt(jnp.sqrt(fourth))
    fourth_scalar = jnp.sum(fourth)
    steps = jnp.int32(3)
    for k in range(1, 8):
        steps = steps + (fourth_scalar > 2.25 ** (4 * k)).astype(jnp.int32)
    extra = (fourth_scalar > 48.0**4).astype(jnp.int32)

    b0 = unit * scale
    t0 = factor(b0)
    b_ref[...] = mm(mm(t0, b0.astype(BF16)).astype(BF16), t0, ABT)
    x_ref[...] = t0.astype(F32) * jnp.sqrt(scale)

    def step(_, carry):
        b = b_ref[...]
        t = factor(b)
        y = mm(t, b.astype(BF16))
        x = mm(t, x_ref[...].astype(BF16))
        b_ref[...] = mm(y.astype(BF16), t, ABT)
        x_ref[...] = x
        return carry

    lax.fori_loop(1, steps, step, 0)

    def error(x):
        y = split(mm3(x, (g_ref[0], g_ref[1])))
        return half(mm3(y, x, ABT) - diag.astype(F32))

    def fix(_, carry):
        x = split(x_ref[...])
        x_ref[...] = x_ref[...] - mm3(split(error(x)), x)
        return carry

    lax.fori_loop(0, extra, fix, 0)
    x = split(x_ref[...])
    z = mm3(x, rhs)
    out = z - mm(error(x).astype(BF16), z.astype(BF16))
    out_ref[...] = out
    send_ref[...] = out.astype(BF16)


def total(value):
    return jnp.sum(jnp.sum(value, axis=1, keepdims=True), axis=0, keepdims=True)


def leaf_kernel(s_ref, u_ref, out_ref, *refs):
    s, u = s_ref[...], u_ref[...]
    wide = s.astype(F32)
    whiten(mm(s, s, ATB), total(wide * wide), mm(s, u, ATB), out_ref, *refs)


def merge_kernel(p_ref, q_ref, out_ref, *refs):
    p, q = p_ref[...], q_ref[...]
    wide = q.astype(F32)
    squares = total(p * p + wide * wide)
    high, low = split(p)
    gram = mm3((high, low), (high, low), ATB) + mm(q, q, ATB)
    cross = mm(high, q, ATB) + mm(low, q, ATB)
    whiten(gram, squares, cross + cross.T, out_ref, *refs)


def dense_call(kernel, left, right):
    width = left.shape[1]
    whole = pl.BlockSpec(memory_space=pltpu.VMEM)
    return pl.pallas_call(
        kernel,
        out_shape=(jax.ShapeDtypeStruct((width, width), F32), jax.ShapeDtypeStruct((width, width), BF16)),
        in_specs=[whole, whole],
        out_specs=(whole, whole),
        scratch_shapes=[
            pltpu.VMEM((width, width), F32),
            pltpu.VMEM((width, width), F32),
            pltpu.VMEM((2, width, width), BF16),
        ],
    )(left, right)


def from_partner(value, axis, distance):
    mask = 2**distance
    pairs = [(source, source ^ mask) for source in range(lax.axis_size(axis))]
    return lax.ppermute(value, axis, pairs)


def iota(shape, axis):
    return lax.broadcasted_iota(jnp.int32, shape, axis)


def one_hot(condition):
    return jnp.where(condition, 1.0, 0.0).astype(BF16)


def column_of(row):
    n = row.shape[1]
    eye = one_hot(iota((n, n), 0) == iota((n, n), 1))
    return mm(eye, jnp.broadcast_to(row, (n, n)).astype(BF16), ABT)


def spread_matrix(leaf_row, tree_row, place_of_slot, slot_rank):
    n = leaf_row.shape[1]
    slots = place_of_slot.shape[0]
    here = leaf_row.astype(F32)
    twin = jnp.where((column_of(leaf_row) == here) & (iota((n, n), 0) < iota((n, n), 1)), 1.0, 0.0)
    rank = jnp.sum(twin, axis=0, keepdims=True)
    pick = one_hot(place_of_slot == iota((slots, n), 1))
    named = mm(pick, jnp.broadcast_to(tree_row, (n, n)).astype(BF16), ABT)
    return one_hot((named == here) & (slot_rank.astype(F32) == rank))


def sample_kernel(
    rows_n, cols_n, a_hbm, right_hbm, left_hbm, leaf_ref, tree_ref, s_out, u_out,
    a_buf, right_buf, left_buf, off_buf, fs, fr, back, bs, bp, bsum, br,
    f1s, f1r, f2s, f2r, b1s, b1r, b2s, b2r,
    in_sem, fs_sem, fr_sem, ps_sem, pr_sem, bs_sem, br_sem,
    f1s_sem, f1r_sem, f2s_sem, f2r_sem, b1s_sem, b1r_sem, b2s_sem, b2r_sem,
):
    i, j = lax.axis_index("row"), lax.axis_index("col")
    lanes = fs.shape[1]
    group = cols_n // 4
    step_rows = group * lanes
    y0 = j // group
    x0, core = i // 2, i % 2
    mesh_id = pl.DeviceIdType.MESH

    def remote(src, dst, send_sem, recv_sem, device):
        return pltpu.make_async_remote_copy(
            src_ref=src, dst_ref=dst, send_sem=send_sem, recv_sem=recv_sem, device_id=device, device_id_type=mesh_id
        )

    barrier = pltpu.get_barrier_semaphore()

    def greet_col(k, _):
        pl.semaphore_signal(barrier, inc=1, device_id={"col": (j + k) % cols_n}, device_id_type=mesh_id)
        return _

    def greet_row(k, _):
        pl.semaphore_signal(barrier, inc=1, device_id={"row": (i + k) % rows_n}, device_id_type=mesh_id)
        return _

    lax.fori_loop(1, cols_n, greet_col, 0)
    lax.fori_loop(1, rows_n, greet_row, 0)

    right_copy = pltpu.make_async_copy(right_hbm, right_buf, in_sem.at[4])
    left_copy = pltpu.make_async_copy(left_hbm, left_buf, in_sem.at[5])

    def rows_at(t):
        return pl.ds(pl.multiple_of(((y0 + 1 + t) % 4) * step_rows, step_rows), step_rows)

    def a_copy(t):
        return pltpu.make_async_copy(a_hbm.at[rows_at(t)], a_buf.at[rows_at(t)], in_sem.at[t])

    a_copy(0).start()
    right_copy.start()
    left_copy.start()
    for t in range(1, 4):
        a_copy(t).start()
    back[...] = jnp.zeros_like(back)
    right_copy.wait()
    left_copy.wait()
    pl.semaphore_wait(barrier, cols_n + rows_n - 2)
    tiles = a_buf.shape[1] // lanes

    def compute(t, carry):
        a_copy(t).wait()
        y = (y0 + 1 + t) % 4
        base = pl.multiple_of(y * step_rows, step_rows)
        for k in range(group):
            mine = column_of(leaf_ref[pl.ds(i * cols_n + y * group + k, 1), :]).astype(BF16)
            for c in range(tiles):
                theirs = leaf_ref[pl.ds(j * rows_n + c, 1), :].astype(BF16)
                block = a_buf[pl.ds(pl.multiple_of(base + k * lanes, lanes), lanes), c * lanes : (c + 1) * lanes]
                off_buf[k * lanes : (k + 1) * lanes, c * lanes : (c + 1) * lanes] = jnp.where(
                    mine == theirs, jnp.zeros_like(block), block
                )
        off = off_buf[...]
        forward = mm(off, right_buf[...]).astype(BF16)
        fs[pl.ds(y * group, group)] = forward.reshape(group, lanes, forward.shape[1])
        for k in range(group):
            peer = y * group + (j + k) % group

            @pl.when(peer != j)
            def _():
                remote(fs.at[peer], fr.at[j], fs_sem.at[peer], fr_sem.at[j], {"col": peer}).start()

        back[...] += mm(left_buf[pl.ds(base, step_rows), :], off, ATB)
        return carry

    lax.fori_loop(0, 4, compute, 0)
    fr[pl.ds(j, 1)] = fs[pl.ds(j, 1)]

    for k in range(rows_n):
        bs[k % 2, k // 2] = back[:, k * lanes : (k + 1) * lanes]
    other = 1 - core
    chips = rows_n // 2

    def pair(k):
        x = (x0 + 1 + k) % chips
        return x, remote(bs.at[other, x], bp.at[x], ps_sem.at[x], pr_sem.at[x], {"row": x0 * 2 + other})

    def pair_start(k, carry):
        pair(k)[1].start()
        return carry

    lax.fori_loop(0, chips, pair_start, 0)

    def along(x):
        return remote(bsum.at[x], br.at[x0], bs_sem.at[x], br_sem.at[x0], {"row": x * 2 + core})

    def pair_end(k, carry):
        x, copy = pair(k)
        copy.wait()
        bsum[pl.ds(x, 1)] = bs[core, pl.ds(x, 1)] + bp[pl.ds(x, 1)]

        @pl.when(x != x0)
        def _():
            along(x).start()

        return carry

    lax.fori_loop(0, chips, pair_end, 0)

    tree = tree_ref[...]
    slots = s_out.shape[0]
    slot = iota((slots, lanes), 0)
    f_place = (slot // 2 % rows_n) * cols_n + slot // (2 * rows_n)
    forward_map = spread_matrix(leaf_ref[pl.ds(i * cols_n + j, 1), :], tree, f_place, slot % 2)
    backward_map = spread_matrix(leaf_ref[pl.ds(j * rows_n + i, 1), :], tree, slot // 2, slot % 2)

    def along_end(k, carry):
        x = (x0 + 1 + k) % chips
        along(x).wait_send()
        remote(bsum.at[x], br.at[x], bs_sem.at[x], br_sem.at[x], {"row": x * 2 + core}).wait_recv()
        return carry

    lax.fori_loop(0, chips - 1, along_end, 0)
    br[pl.ds(x0, 1)] = bsum[pl.ds(x0, 1)]
    sample_back = jnp.sum(br[...], axis=0).astype(BF16)
    width = s_out.shape[1]

    def rows_exchange(src, dst, send_sem, recv_sem):
        def start(k, carry):
            peer = (i + k) % rows_n
            remote(src.at[peer], dst.at[i], send_sem.at[peer], recv_sem.at[i], {"row": peer}).start()
            return carry

        def end(k, carry):
            peer = (i + k) % rows_n
            remote(src.at[peer], dst.at[peer], send_sem.at[peer], recv_sem.at[peer], {"row": peer}).wait()
            return carry

        return start, end

    def cols_exchange(src, dst, send_sem, recv_sem):
        def start(k, carry):
            peer = (j + k) % cols_n
            remote(src.at[peer], dst.at[j], send_sem.at[peer], recv_sem.at[j], {"col": peer}).start()
            return carry

        def end(k, carry):
            peer = (j + k) % cols_n
            remote(src.at[peer], dst.at[peer], send_sem.at[peer], recv_sem.at[peer], {"col": peer}).wait()
            return carry

        return start, end

    b1_start, b1_end = rows_exchange(b1s, b1r, b1s_sem, b1r_sem)
    b2_start, b2_end = cols_exchange(b2s, b2r, b2s_sem, b2r_sem)
    f1_start, f1_end = cols_exchange(f1s, f1r, f1s_sem, f1r_sem)
    f2_start, f2_end = rows_exchange(f2s, f2r, f2s_sem, f2r_sem)
    f0_end = cols_exchange(fs, fr, fs_sem, fr_sem)[1]

    b1s[...] = mm(backward_map, sample_back, ABT).astype(BF16).reshape(b1s.shape)
    lax.fori_loop(1, rows_n, b1_start, 0)
    b1r[pl.ds(i, 1)] = b1s[pl.ds(i, 1)]

    lax.fori_loop(1, cols_n, f0_end, 0)
    forward_sum = fr[0].astype(F32)
    for k in range(1, cols_n):
        forward_sum += fr[k].astype(F32)
    f1s[...] = mm(forward_map, forward_sum.astype(BF16)).astype(BF16).reshape(f1s.shape)
    lax.fori_loop(1, cols_n, f1_start, 0)
    f1r[pl.ds(j, 1)] = f1s[pl.ds(j, 1)]

    slot = iota((slots, slots), 0)
    source = iota((slots, slots), 1)
    row_col = (slot // 2 % cols_n) * (2 * rows_n) + (slot // (2 * cols_n)) * 2 + slot % 2
    col_row = (slot // 2 % rows_n) * (2 * cols_n) + (slot // (2 * rows_n)) * 2 + slot % 2
    to_rows, to_cols = one_hot(source == row_col), one_hot(source == col_row)

    lax.fori_loop(1, rows_n, b1_end, 0)
    b2s[...] = mm(to_cols, b1r[...].reshape(slots, width)).astype(BF16).reshape(b2s.shape)
    lax.fori_loop(1, cols_n, b2_start, 0)
    b2r[pl.ds(j, 1)] = b2s[pl.ds(j, 1)]

    lax.fori_loop(1, cols_n, f1_end, 0)
    f2s[...] = mm(to_rows, f1r[...].reshape(slots, width)).astype(BF16).reshape(f2s.shape)
    lax.fori_loop(1, rows_n, f2_start, 0)
    f2r[pl.ds(i, 1)] = f2s[pl.ds(i, 1)]

    lax.fori_loop(1, cols_n, b2_end, 0)
    u_out[...] = b2r[...].reshape(slots, width)
    lax.fori_loop(1, rows_n, f2_end, 0)
    s_out[...] = f2r[...].reshape(slots, width)


def sample_call(front_block, probe_right, probe_left, leaves, tree, rows_n, cols_n):
    tile_rows, tile_cols = front_block.shape
    samples = probe_right.shape[1]
    lanes = leaves.shape[1]
    slots = 2 * rows_n * cols_n
    chips = rows_n // 2
    vmem = pl.BlockSpec(memory_space=pltpu.VMEM)
    hbm = pl.BlockSpec(memory_space=pl.ANY)
    out = jax.ShapeDtypeStruct((slots, samples), BF16)
    by_col = pltpu.VMEM((cols_n, 2 * rows_n, samples), BF16)
    by_row = pltpu.VMEM((rows_n, 2 * cols_n, samples), BF16)
    dma = pltpu.SemaphoreType.DMA
    return pl.pallas_call(
        functools.partial(sample_kernel, rows_n, cols_n),
        out_shape=(out, out),
        in_specs=[hbm, hbm, hbm, vmem, vmem],
        out_specs=(vmem, vmem),
        scratch_shapes=[
            pltpu.VMEM((tile_rows, tile_cols), BF16),
            pltpu.VMEM((tile_cols, samples), BF16),
            pltpu.VMEM((tile_rows, samples), BF16),
            pltpu.VMEM((tile_rows // 4, tile_cols), BF16),
            pltpu.VMEM((cols_n, lanes, samples), BF16),
            pltpu.VMEM((cols_n, lanes, samples), BF16),
            pltpu.VMEM((samples, tile_cols), F32),
            pltpu.VMEM((2, chips, samples, lanes), F32),
            pltpu.VMEM((chips, samples, lanes), F32),
            pltpu.VMEM((chips, samples, lanes), F32),
            pltpu.VMEM((chips, samples, lanes), F32),
            by_col, by_col, by_row, by_row, by_row, by_row, by_col, by_col,
            dma((6,)),
            dma((cols_n,)), dma((cols_n,)),
            dma((chips,)), dma((chips,)), dma((chips,)), dma((chips,)),
            dma((cols_n,)), dma((cols_n,)), dma((rows_n,)), dma((rows_n,)),
            dma((rows_n,)), dma((rows_n,)), dma((cols_n,)), dma((cols_n,)),
        ],
        compiler_params=pltpu.CompilerParams(collective_id=0, has_side_effects=True, vmem_limit_bytes=48 * 2**20),
    )(front_block, probe_right, probe_left, leaves, tree)


def per_device(front_block, probe_right, probe_left, row_leaf, tree_leaf):
    rows_n, cols_n = lax.axis_size("row"), lax.axis_size("col")
    devices = rows_n * cols_n
    leaves = row_leaf.reshape(devices, row_leaf.shape[0] // devices)
    forward_recv, backward_recv = sample_call(
        front_block, probe_right, probe_left, leaves, tree_leaf.reshape(1, devices), rows_n, cols_n
    )
    coupling, sent = dense_call(leaf_kernel, forward_recv, backward_recv)
    merged = coupling
    for level in range(2):
        merged, sent = dense_call(merge_kernel, merged, from_partner(sent, "col", level))
    return (coupling[None], merged[None])


def solution(mesh):
    return jax.shard_map(
        per_device,
        mesh=mesh,
        in_specs=(P("row", "col"), P("col", None), P("row", None), P(), P()),
        out_specs=(P(("row", "col"), None, None), P(("row", "col"), None, None)),
        check_vma=False,
    )
```

```python
import functools

import jax
import jax.numpy as jnp
from jax import lax
from jax.experimental import pallas as pl
from jax.experimental.pallas import tpu as pltpu
from jax.sharding import PartitionSpec as P

eps = 1e-05
F32, BF16 = jnp.float32, jnp.bfloat16
AB = (((1,), (0,)), ((), ()))
ABT = (((1,), (1,)), ((), ()))
ATB = (((0,), (0,)), ((), ()))


def split(value):
    high = value.astype(BF16)
    return high, (value - high.astype(F32)).astype(BF16)


def mm(left, right, dims=AB):
    return lax.dot_general(left, right, dims, preferred_element_type=F32)


def mm3(left, right, dims=AB):
    return mm(left[0], right[0], dims) + (mm(left[0], right[1], dims) + mm(left[1], right[0], dims))


def whiten(problems, b_ref, x_ref, g_ref):
    width = problems[0][0].shape[0]
    row = lax.broadcasted_iota(jnp.int32, (width, width), 0)
    col = lax.broadcasted_iota(jnp.int32, (width, width), 1)
    below, diag = row > col, row == col

    def half(value):
        return jnp.where(below, value, jnp.where(diag, 0.5 * value, 0.0))

    def factor(value):
        return jnp.where(below, -value, jnp.where(diag, 1.5 - 0.5 * value, 0.0)).astype(BF16)

    def step(b, x, growth):
        b = b * growth
        t = factor(b)
        y = mm(t, b.astype(BF16))
        return mm(y.astype(BF16), t, ABT), mm(t, (x * growth**0.5).astype(BF16))

    def error(x, n):
        y = split(mm3(x, (g_ref[n, 0], g_ref[n, 1])))
        return half(mm3(y, x, ABT) - diag.astype(F32))

    rhs, worst, states = [], None, []
    for n, (gram, squares, cross) in enumerate(problems):
        ridge = squares / width + eps
        inv_root = lax.rsqrt(ridge)
        unit = gram * (inv_root * inv_root) + diag.astype(F32)
        g_ref[n, 0], g_ref[n, 1] = split(unit)
        rhs.append(split(cross * inv_root))
        high = unit.astype(BF16)
        square = mm(high, high)
        fourth = total(square * square)
        worst = fourth if worst is None else jnp.maximum(worst, fourth)
        scale = 1.9 * lax.rsqrt(jnp.sqrt(fourth))
        b = unit * scale
        t = factor(b)
        states.append((mm(mm(t, b.astype(BF16)).astype(BF16), t, ABT), t.astype(F32) * jnp.sqrt(scale)))
    worst = jnp.sum(worst)
    steps = jnp.int32(4)
    for bound in (20.0, 45.0, 100.0, 180.0):
        steps = steps + (worst > bound**4).astype(jnp.int32)
    extra = (worst > 48.0**4).astype(jnp.int32)

    for growth in (1.3, 1.2, 1.0):
        states = [step(b, x, growth) for b, x in states]
    for n, (b, x) in enumerate(states):
        b_ref[n] = b
        x_ref[n] = x

    def more(_, carry):
        for n in range(len(problems)):
            b_ref[n], x_ref[n] = step(b_ref[n], x_ref[n], 1.0)
        return carry

    def fix(_, carry):
        for n in range(len(problems)):
            x = split(x_ref[n])
            x_ref[n] = x_ref[n] - mm3(split(error(x, n)), x)
        return carry

    lax.fori_loop(4, steps, more, 0)
    lax.fori_loop(0, extra, fix, 0)
    outs = []
    for n in range(len(problems)):
        x = split(x_ref[n])
        z = mm3(x, rhs[n])
        outs.append(z - mm(error(x, n).astype(BF16), z.astype(BF16)))
    return outs


def total(value):
    return jnp.sum(jnp.sum(value, axis=1, keepdims=True), axis=0, keepdims=True)


def leaf_kernel(s_ref, u_ref, out_ref, send_ref, *refs):
    s, u = s_ref[...], u_ref[...]
    wide = s.astype(F32)
    (out,) = whiten([(mm(s, s, ATB), total(wide * wide), mm(s, u, ATB))], *refs)
    out_ref[...] = out
    send_ref[...] = out.astype(BF16)


def merge_parts(p, q):
    gram, squares = 0.0, 0.0
    for high, low in (p, q):
        if low is None:
            wide = high.astype(F32)
            gram += mm(high, high, ATB)
        else:
            wide = high.astype(F32) + low.astype(F32)
            gram += mm3((high, low), (high, low), ATB)
        squares += total(wide * wide)
    cross = mm(p[0], q[0], ATB)
    if p[1] is not None:
        cross += mm(p[1], q[0], ATB)
    if q[1] is not None:
        cross += mm(p[0], q[1], ATB)
    return gram, squares, cross + cross.T


def merge_kernel(p_ref, q1_ref, q2_ref, q3_ref, out_ref, *refs):
    near, far = whiten(
        [
            merge_parts(split(p_ref[...]), (q1_ref[...], None)),
            merge_parts((q2_ref[...], None), (q3_ref[...], None)),
        ],
        *refs,
    )
    (out_ref[...],) = whiten([merge_parts(split(near), split(far))], *refs)


def dense_call(kernel, out_shapes, problems, *args):
    width = args[0].shape[1]
    whole = pl.BlockSpec(memory_space=pltpu.VMEM)
    return pl.pallas_call(
        kernel,
        out_shape=tuple(jax.ShapeDtypeStruct((width, width), dtype) for dtype in out_shapes),
        in_specs=[whole] * len(args),
        out_specs=(whole,) * len(out_shapes),
        scratch_shapes=[
            pltpu.VMEM((problems, width, width), F32),
            pltpu.VMEM((problems, width, width), F32),
            pltpu.VMEM((problems, 2, width, width), BF16),
        ],
        compiler_params=pltpu.CompilerParams(vmem_limit_bytes=16 * 2**20),
    )(*args)


def from_partner(value, axis, mask):
    pairs = [(source, source ^ mask) for source in range(lax.axis_size(axis))]
    return lax.ppermute(value, axis, pairs)


def iota(shape, axis):
    return lax.broadcasted_iota(jnp.int32, shape, axis)


def one_hot(condition):
    return jnp.where(condition, 1.0, 0.0).astype(BF16)


def column_of(row):
    n = row.shape[1]
    eye = one_hot(iota((n, n), 0) == iota((n, n), 1))
    return mm(eye, jnp.broadcast_to(row, (n, n)).astype(BF16), ABT)


def spread_matrix(leaf_row, tree_row, place_of_slot, slot_rank):
    n = leaf_row.shape[1]
    slots = place_of_slot.shape[0]
    here = leaf_row.astype(F32)
    twin = jnp.where((column_of(leaf_row) == here) & (iota((n, n), 0) < iota((n, n), 1)), 1.0, 0.0)
    rank = jnp.sum(twin, axis=0, keepdims=True)
    pick = one_hot(place_of_slot == iota((slots, n), 1))
    named = mm(pick, jnp.broadcast_to(tree_row, (n, n)).astype(BF16), ABT)
    return one_hot((named == here) & (slot_rank.astype(F32) == rank))


def sample_kernel(
    rows_n, cols_n, a_hbm, right_hbm, left_hbm, leaf_hbm, tree_hbm, s_out, u_out,
    leaf_ref, tree_ref, a_buf, right_buf, left_buf, fs, fr, back, bs, bp, bsum, br,
    f1s, f1r, f2s, f2r, b1s, b1r, b2s, b2r,
    in_sem, fs_sem, fr_sem, ps_sem, pr_sem, bs_sem, br_sem,
    f1s_sem, f1r_sem, f2s_sem, f2r_sem, b1s_sem, b1r_sem, b2s_sem, b2r_sem,
):
    i, j = lax.axis_index("row"), lax.axis_index("col")
    lanes = fs.shape[1]
    group = cols_n // 4
    step_rows = group * lanes
    y0 = j // group
    x0, core = i // 2, i % 2
    mesh_id = pl.DeviceIdType.MESH

    def remote(src, dst, send_sem, recv_sem, device):
        return pltpu.make_async_remote_copy(
            src_ref=src, dst_ref=dst, send_sem=send_sem, recv_sem=recv_sem, device_id=device, device_id_type=mesh_id
        )

    barrier = pltpu.get_barrier_semaphore()

    def greet_col(k, _):
        pl.semaphore_signal(barrier, inc=1, device_id={"col": (j + k) % cols_n}, device_id_type=mesh_id)
        return _

    def greet_row(k, _):
        pl.semaphore_signal(barrier, inc=1, device_id={"row": (i + k) % rows_n}, device_id_type=mesh_id)
        return _

    lax.fori_loop(1, cols_n, greet_col, 0)
    lax.fori_loop(1, rows_n, greet_row, 0)

    right_copy = pltpu.make_async_copy(right_hbm, right_buf, in_sem.at[4])
    left_copy = pltpu.make_async_copy(left_hbm, left_buf, in_sem.at[5])
    leaf_copy = pltpu.make_async_copy(leaf_hbm, leaf_ref, in_sem.at[6])
    tree_copy = pltpu.make_async_copy(tree_hbm, tree_ref, in_sem.at[7])

    def rows_at(t):
        return pl.ds(pl.multiple_of(((y0 + 1 + t) % 4) * step_rows, step_rows), step_rows)

    def a_copy(t):
        return pltpu.make_async_copy(a_hbm.at[rows_at(t)], a_buf.at[rows_at(t)], in_sem.at[t])

    leaf_copy.start()
    tree_copy.start()
    left_copy.start()
    for t in range(4):
        a_copy(t).start()
    right_copy.start()
    leaf_copy.wait()
    tree_copy.wait()
    tiles = a_buf.shape[1] // lanes
    for t in range(4):
        a_copy(t).wait()
        if t == 0:
            left_copy.wait()
        base = pl.multiple_of(((y0 + 1 + t) % 4) * step_rows, step_rows)
        for k in range(group):
            mine = column_of(leaf_ref[pl.ds(i * cols_n + base // lanes + k, 1), :]).astype(BF16)
            rows = pl.ds(pl.multiple_of(base + k * lanes, lanes), lanes)
            for c in range(tiles):
                theirs = leaf_ref[pl.ds(j * rows_n + c, 1), :].astype(BF16)
                block = a_buf[rows, c * lanes : (c + 1) * lanes]
                a_buf[rows, c * lanes : (c + 1) * lanes] = jnp.where(mine == theirs, jnp.zeros_like(block), block)
        part = mm(left_buf[pl.ds(base, step_rows), :], a_buf[pl.ds(base, step_rows), :], ATB)
        if t == 0:
            back[...] = part
        elif t < 3:
            back[...] += part
        else:
            part += back[...]
            for k in range(rows_n):
                bs[k % 2, k // 2] = part[:, k * lanes : (k + 1) * lanes]
    pl.semaphore_wait(barrier, cols_n + rows_n - 2)
    other = 1 - core
    chips = rows_n // 2

    def pair(k):
        x = (x0 + 1 + k) % chips
        return x, remote(bs.at[other, x], bp.at[x], ps_sem.at[x], pr_sem.at[x], {"row": x0 * 2 + other})

    def pair_start(k, carry):
        pair(k)[1].start()
        return carry

    lax.fori_loop(0, chips, pair_start, 0)
    right_copy.wait()

    def compute(t, carry):
        y = (y0 + 1 + t) % 4
        base = pl.multiple_of(y * step_rows, step_rows)
        forward = mm(a_buf[pl.ds(base, step_rows), :], right_buf[...]).astype(BF16)
        fs[pl.ds(y * group, group)] = forward.reshape(group, lanes, forward.shape[1])
        for k in range(group):
            peer = y * group + (j + k) % group

            @pl.when(peer != j)
            def _():
                remote(fs.at[peer], fr.at[j], fs_sem.at[peer], fr_sem.at[j], {"col": peer}).start()

        return carry

    lax.fori_loop(0, 4, compute, 0)
    fr[pl.ds(j, 1)] = fs[pl.ds(j, 1)]

    def along(x):
        return remote(bsum.at[x], br.at[x0], bs_sem.at[x], br_sem.at[x0], {"row": x * 2 + core})

    def pair_end(k, carry):
        x, copy = pair(k)
        copy.wait()
        bsum[pl.ds(x, 1)] = bs[core, pl.ds(x, 1)] + bp[pl.ds(x, 1)]

        @pl.when(x != x0)
        def _():
            along(x).start()

        return carry

    lax.fori_loop(0, chips, pair_end, 0)

    tree = tree_ref[...]
    slots = s_out.shape[0]
    slot = iota((slots, lanes), 0)
    row_bits, col_bits = rows_n.bit_length() - 1, cols_n.bit_length() - 1
    f_place = (((slot >> 1) & (rows_n - 1)) << col_bits) + (slot >> (1 + row_bits))
    forward_map = spread_matrix(leaf_ref[pl.ds(i * cols_n + j, 1), :], tree, f_place, slot & 1)
    backward_map = spread_matrix(leaf_ref[pl.ds(j * rows_n + i, 1), :], tree, slot >> 1, slot & 1)

    def along_end(k, carry):
        x = (x0 + 1 + k) % chips
        along(x).wait_send()
        remote(bsum.at[x], br.at[x], bs_sem.at[x], br_sem.at[x], {"row": x * 2 + core}).wait_recv()
        return carry

    lax.fori_loop(0, chips - 1, along_end, 0)
    br[pl.ds(x0, 1)] = bsum[pl.ds(x0, 1)]
    sample_back = jnp.sum(br[...], axis=0).astype(BF16)
    width = s_out.shape[1]

    def rows_exchange(src, dst, send_sem, recv_sem):
        def start(k, carry):
            peer = (i + k) % rows_n
            remote(src.at[peer], dst.at[i], send_sem.at[peer], recv_sem.at[i], {"row": peer}).start()
            return carry

        def end(k, carry):
            peer = (i + k) % rows_n
            remote(src.at[peer], dst.at[peer], send_sem.at[peer], recv_sem.at[peer], {"row": peer}).wait()
            return carry

        return start, end

    def cols_exchange(src, dst, send_sem, recv_sem):
        def start(k, carry):
            peer = (j + k) % cols_n
            remote(src.at[peer], dst.at[j], send_sem.at[peer], recv_sem.at[j], {"col": peer}).start()
            return carry

        def end(k, carry):
            peer = (j + k) % cols_n
            remote(src.at[peer], dst.at[peer], send_sem.at[peer], recv_sem.at[peer], {"col": peer}).wait()
            return carry

        return start, end

    b1_start, b1_end = rows_exchange(b1s, b1r, b1s_sem, b1r_sem)
    b2_start, b2_end = cols_exchange(b2s, b2r, b2s_sem, b2r_sem)
    f1_start, f1_end = cols_exchange(f1s, f1r, f1s_sem, f1r_sem)
    f2_start, f2_end = rows_exchange(f2s, f2r, f2s_sem, f2r_sem)
    f0_end = cols_exchange(fs, fr, fs_sem, fr_sem)[1]

    b1s[...] = mm(backward_map, sample_back, ABT).astype(BF16).reshape(b1s.shape)
    lax.fori_loop(1, rows_n, b1_start, 0)
    b1r[pl.ds(i, 1)] = b1s[pl.ds(i, 1)]

    lax.fori_loop(1, cols_n, f0_end, 0)
    forward_sum = fr[0].astype(F32)
    for k in range(1, cols_n):
        forward_sum += fr[k].astype(F32)
    f1s[...] = mm(forward_map, forward_sum.astype(BF16)).astype(BF16).reshape(f1s.shape)
    lax.fori_loop(1, cols_n, f1_start, 0)
    f1r[pl.ds(j, 1)] = f1s[pl.ds(j, 1)]

    slot = iota((slots, slots), 0)
    source = iota((slots, slots), 1)
    row_col = (((slot >> 1) & (cols_n - 1)) << (1 + row_bits)) + ((slot >> (1 + col_bits)) << 1) + (slot & 1)
    col_row = (((slot >> 1) & (rows_n - 1)) << (1 + col_bits)) + ((slot >> (1 + row_bits)) << 1) + (slot & 1)
    to_rows, to_cols = one_hot(source == row_col), one_hot(source == col_row)

    lax.fori_loop(1, rows_n, b1_end, 0)
    b2s[...] = mm(to_cols, b1r[...].reshape(slots, width)).astype(BF16).reshape(b2s.shape)
    lax.fori_loop(1, cols_n, b2_start, 0)
    b2r[pl.ds(j, 1)] = b2s[pl.ds(j, 1)]

    lax.fori_loop(1, cols_n, f1_end, 0)
    f2s[...] = mm(to_rows, f1r[...].reshape(slots, width)).astype(BF16).reshape(f2s.shape)
    lax.fori_loop(1, rows_n, f2_start, 0)
    f2r[pl.ds(i, 1)] = f2s[pl.ds(i, 1)]

    lax.fori_loop(1, cols_n, b2_end, 0)
    u_out[...] = b2r[...].reshape(slots, width)
    lax.fori_loop(1, rows_n, f2_end, 0)
    s_out[...] = f2r[...].reshape(slots, width)


def sample_call(front_block, probe_right, probe_left, leaves, tree, rows_n, cols_n):
    tile_rows, tile_cols = front_block.shape
    samples = probe_right.shape[1]
    lanes = leaves.shape[1]
    slots = 2 * rows_n * cols_n
    chips = rows_n // 2
    vmem = pl.BlockSpec(memory_space=pltpu.VMEM)
    hbm = pl.BlockSpec(memory_space=pltpu.HBM)
    out = jax.ShapeDtypeStruct((slots, samples), BF16)
    by_col = pltpu.VMEM((cols_n, 2 * rows_n, samples), BF16)
    by_row = pltpu.VMEM((rows_n, 2 * cols_n, samples), BF16)
    dma = pltpu.SemaphoreType.DMA
    return pl.pallas_call(
        functools.partial(sample_kernel, rows_n, cols_n),
        out_shape=(out, out),
        in_specs=[hbm] * 5,
        out_specs=(vmem, vmem),
        scratch_shapes=[
            pltpu.VMEM(leaves.shape, jnp.int32),
            pltpu.VMEM(tree.shape, jnp.int32),
            pltpu.VMEM((tile_rows, tile_cols), BF16),
            pltpu.VMEM((tile_cols, samples), BF16),
            pltpu.VMEM((tile_rows, samples), BF16),
            pltpu.VMEM((cols_n, lanes, samples), BF16),
            pltpu.VMEM((cols_n, lanes, samples), BF16),
            pltpu.VMEM((samples, tile_cols), F32),
            pltpu.VMEM((2, chips, samples, lanes), F32),
            pltpu.VMEM((chips, samples, lanes), F32),
            pltpu.VMEM((chips, samples, lanes), F32),
            pltpu.VMEM((chips, samples, lanes), F32),
            by_col, by_col, by_row, by_row, by_row, by_row, by_col, by_col,
            dma((8,)),
            dma((cols_n,)), dma((cols_n,)),
            dma((chips,)), dma((chips,)), dma((chips,)), dma((chips,)),
            dma((cols_n,)), dma((cols_n,)), dma((rows_n,)), dma((rows_n,)),
            dma((rows_n,)), dma((rows_n,)), dma((cols_n,)), dma((cols_n,)),
        ],
        compiler_params=pltpu.CompilerParams(collective_id=0, has_side_effects=True, vmem_limit_bytes=67043328),
    )(front_block, probe_right, probe_left, leaves, tree)


def per_device(front_block, probe_right, probe_left, row_leaf, tree_leaf):
    rows_n, cols_n = lax.axis_size("row"), lax.axis_size("col")
    devices = rows_n * cols_n
    leaves = row_leaf.reshape(devices, row_leaf.shape[0] // devices)
    forward_recv, backward_recv = sample_call(
        front_block, probe_right, probe_left, leaves, tree_leaf.reshape(1, devices), rows_n, cols_n
    )
    coupling, sent = dense_call(leaf_kernel, (F32, BF16), 1, forward_recv, backward_recv)
    others = [from_partner(sent, "col", mask) for mask in (1, 2, 3)]
    (merged,) = dense_call(merge_kernel, (F32,), 2, coupling, *others)
    return (coupling[None], merged[None])


def solution(mesh):
    return jax.shard_map(
        per_device,
        mesh=mesh,
        in_specs=(P("row", "col"), P("col", None), P("row", None), P(), P()),
        out_specs=(P(("row", "col"), None, None), P(("row", "col"), None, None)),
        check_vma=False,
    )
```

```python
import functools

import jax
import jax.numpy as jnp
from jax import lax
from jax.experimental import pallas as pl
from jax.experimental.pallas import tpu as pltpu
from jax.sharding import PartitionSpec as P

eps = 1e-05
F32, BF16 = jnp.float32, jnp.bfloat16
AB = (((1,), (0,)), ((), ()))
ABT = (((1,), (1,)), ((), ()))
ATB = (((0,), (0,)), ((), ()))


def split(value):
    high = value.astype(BF16)
    return high, (value - high.astype(F32)).astype(BF16)


def mm(left, right, dims=AB):
    return lax.dot_general(left, right, dims, preferred_element_type=F32)


def mm3(left, right, dims=AB):
    return mm(left[0], right[0], dims) + (mm(left[0], right[1], dims) + mm(left[1], right[0], dims))


def whiten(problems, b_ref, x_ref, g_ref):
    width = problems[0][0].shape[0]
    row = lax.broadcasted_iota(jnp.int32, (width, width), 0)
    col = lax.broadcasted_iota(jnp.int32, (width, width), 1)
    below, diag = row > col, row == col

    def half(value):
        return jnp.where(below, value, jnp.where(diag, 0.5 * value, 0.0))

    def factor(value):
        return jnp.where(below, -value, jnp.where(diag, 1.5 - 0.5 * value, 0.0)).astype(BF16)

    def step(b, x, growth):
        b = b * growth
        t = factor(b)
        y = mm(t, b.astype(BF16))
        return mm(y.astype(BF16), t, ABT), mm(t, (x * growth**0.5).astype(BF16))

    def error(x, n):
        y = split(mm3(x, (g_ref[n, 0], g_ref[n, 1])))
        return half(mm3(y, x, ABT) - diag.astype(F32))

    rhs, worst, states = [], None, []
    for n, (gram, squares, cross) in enumerate(problems):
        ridge = squares / width + eps
        inv_root = lax.rsqrt(ridge)
        unit = gram * (inv_root * inv_root) + diag.astype(F32)
        g_ref[n, 0], g_ref[n, 1] = split(unit)
        rhs.append(split(cross * inv_root))
        high = unit.astype(BF16)
        square = mm(high, high)
        fourth = total(square * square)
        worst = fourth if worst is None else jnp.maximum(worst, fourth)
        scale = 1.9 * lax.rsqrt(jnp.sqrt(fourth))
        b = unit * scale
        t = factor(b)
        states.append((mm(mm(t, b.astype(BF16)).astype(BF16), t, ABT), t.astype(F32) * jnp.sqrt(scale)))
    worst = jnp.sum(worst)
    steps = jnp.int32(3)
    for bound in (16.0, 24.0, 45.0, 100.0, 180.0):
        steps = steps + (worst > bound**4).astype(jnp.int32)
    extra = (worst > 48.0**4).astype(jnp.int32)

    for growth in (1.3, 1.2):
        states = [step(b, x, growth) for b, x in states]
    for n, (b, x) in enumerate(states):
        b_ref[n] = b
        x_ref[n] = x

    def more(_, carry):
        for n in range(len(problems)):
            b_ref[n], x_ref[n] = step(b_ref[n], x_ref[n], 1.0)
        return carry

    def fix(_, carry):
        for n in range(len(problems)):
            x = split(x_ref[n])
            x_ref[n] = x_ref[n] - mm3(split(error(x, n)), x)
        return carry

    lax.fori_loop(3, steps, more, 0)
    lax.fori_loop(0, extra, fix, 0)
    outs = []
    for n in range(len(problems)):
        x = split(x_ref[n])
        z = mm3(x, rhs[n])
        outs.append(z - mm(error(x, n).astype(BF16), z.astype(BF16)))
    return outs


def total(value):
    return jnp.sum(jnp.sum(value, axis=1, keepdims=True), axis=0, keepdims=True)


def leaf_kernel(rows_ref, out_ref, send_ref, *refs):
    s, u = rows_ref[0], rows_ref[1]
    wide = s.astype(F32)
    s_t = s.T
    (out,) = whiten([(mm(s_t, s), total(wide * wide), mm(s_t, u))], *refs)
    out_ref[...] = out
    send_ref[...] = out.astype(BF16)


def product(left, right):
    out = mm(left[0], right[0])
    if left[1] is not None:
        out += mm(left[1], right[0])
    if right[1] is not None:
        out += mm(left[0], right[1])
    return out


def merge_parts(p, q):
    p_t, q_t = (tuple(None if part is None else part.T for part in node) for node in (p, q))
    squares = 0.0
    for high, low in (p, q):
        wide = high.astype(F32) if low is None else high.astype(F32) + low.astype(F32)
        squares += total(wide * wide)
    return product(p_t, p) + product(q_t, q), squares, product(p_t, q) + product(q_t, p)


def merge_kernel(p_ref, q_ref, out_ref, *refs):
    near, far = whiten(
        [
            merge_parts(split(p_ref[...]), (q_ref[0], None)),
            merge_parts((q_ref[1], None), (q_ref[2], None)),
        ],
        *refs,
    )
    (out_ref[...],) = whiten([merge_parts(split(near), split(far))], *refs)


def dense_call(kernel, out_shapes, problems, *args):
    width = args[0].shape[-1]
    whole = pl.BlockSpec(memory_space=pltpu.VMEM)
    return pl.pallas_call(
        kernel,
        out_shape=tuple(jax.ShapeDtypeStruct((width, width), dtype) for dtype in out_shapes),
        in_specs=[whole] * len(args),
        out_specs=(whole,) * len(out_shapes),
        scratch_shapes=[
            pltpu.VMEM((problems, width, width), F32),
            pltpu.VMEM((problems, width, width), F32),
            pltpu.VMEM((problems, 2, width, width), BF16),
        ],
        compiler_params=pltpu.CompilerParams(vmem_limit_bytes=67043328),
    )(*args)


def gather_kernel(sent, out, send_sem, recv_sem):
    j = lax.axis_index("col")
    z = j % 4
    peers = [j - z + near for near in (z + 1 - 2 * (z % 2), (z + 2) % 4, 3 - z)]
    mesh_id = pl.DeviceIdType.MESH
    barrier = pltpu.get_barrier_semaphore()
    for peer in peers:
        pl.semaphore_signal(barrier, inc=1, device_id={"col": peer}, device_id_type=mesh_id)
    pl.semaphore_wait(barrier, 3)
    copies = [
        pltpu.make_async_remote_copy(
            src_ref=sent, dst_ref=out.at[n], send_sem=send_sem.at[n], recv_sem=recv_sem.at[n],
            device_id={"col": peer}, device_id_type=mesh_id,
        )
        for n, peer in enumerate(peers)
    ]
    for n in (1, 0, 2):
        copies[n].start()
    for copy in copies:
        copy.wait()


def gather_call(sent):
    anywhere = pl.BlockSpec(memory_space=pl.ANY)
    return pl.pallas_call(
        gather_kernel,
        out_shape=jax.ShapeDtypeStruct((3, *sent.shape), sent.dtype),
        in_specs=[anywhere],
        out_specs=anywhere,
        scratch_shapes=[pltpu.SemaphoreType.DMA((3,)), pltpu.SemaphoreType.DMA((3,))],
        compiler_params=pltpu.CompilerParams(collective_id=1, has_side_effects=True, vmem_limit_bytes=67043328),
    )(sent)


def iota(shape, axis):
    return lax.broadcasted_iota(jnp.int32, shape, axis)


def one_hot(condition):
    return jnp.where(condition, 1.0, 0.0).astype(BF16)


def column_of(row):
    n = row.shape[1]
    eye = one_hot(iota((n, n), 0) == iota((n, n), 1))
    return mm(eye, jnp.broadcast_to(row, (n, n)).astype(BF16), ABT)


def spread_matrix(leaf_row, tree_row, place_of_slot, slot_rank):
    n = leaf_row.shape[1]
    slots = place_of_slot.shape[0]
    here = leaf_row.astype(F32)
    twin = jnp.where((column_of(leaf_row) == here) & (iota((n, n), 0) < iota((n, n), 1)), 1.0, 0.0)
    rank = jnp.sum(twin, axis=0, keepdims=True)
    pick = one_hot(place_of_slot == iota((slots, n), 1))
    named = mm(pick, jnp.broadcast_to(tree_row, (n, n)).astype(BF16), ABT)
    return one_hot((named == here) & (slot_rank.astype(F32) == rank))


def sample_kernel(
    rows_n, cols_n, a_hbm, right_hbm, left_hbm, leaf_hbm, tree_hbm, out,
    leaf_ref, tree_ref, a_buf, right_buf, left_buf, fs, fr, back, bs, bp, bsum, br,
    f1s, f1r, f2s, b1s, b1r, b2s, acc,
    in_sem, fs_sem, fr_sem, ps_sem, pr_sem, bs_sem, br_sem,
    f1s_sem, f1r_sem, f2s_sem, f2r_sem, b1s_sem, b1r_sem, b2s_sem, b2r_sem,
):
    i, j = lax.axis_index("row"), lax.axis_index("col")
    lanes = fs.shape[1]
    group = cols_n // 4
    step_rows = group * lanes
    y0, z0 = j // group, j % group
    far_first = (2, 1, 3, 0)
    x0, core = i // 2, i % 2
    mesh_id = pl.DeviceIdType.MESH

    def remote(src, dst, send_sem, recv_sem, device):
        return pltpu.make_async_remote_copy(
            src_ref=src, dst_ref=dst, send_sem=send_sem, recv_sem=recv_sem, device_id=device, device_id_type=mesh_id
        )

    barrier = pltpu.get_barrier_semaphore()

    def greet_col(k, _):
        pl.semaphore_signal(barrier, inc=1, device_id={"col": (j + k) % cols_n}, device_id_type=mesh_id)
        return _

    def greet_row(k, _):
        pl.semaphore_signal(barrier, inc=1, device_id={"row": (i + k) % rows_n}, device_id_type=mesh_id)
        return _

    lax.fori_loop(1, cols_n, greet_col, 0)
    lax.fori_loop(1, rows_n, greet_row, 0)

    right_copy = pltpu.make_async_copy(right_hbm, right_buf, in_sem.at[4])
    left_copy = pltpu.make_async_copy(left_hbm, left_buf, in_sem.at[5])
    leaf_copy = pltpu.make_async_copy(leaf_hbm, leaf_ref, in_sem.at[6])
    tree_copy = pltpu.make_async_copy(tree_hbm, tree_ref, in_sem.at[7])

    def rows_at(t):
        return pl.ds(pl.multiple_of(((y0 + far_first[t]) % 4) * step_rows, step_rows), step_rows)

    def a_copy(t):
        return pltpu.make_async_copy(a_hbm.at[rows_at(t)], a_buf.at[rows_at(t)], in_sem.at[t])

    leaf_copy.start()
    tree_copy.start()
    a_copy(0).start()
    right_copy.start()
    a_copy(1).start()
    left_copy.start()
    a_copy(2).start()
    a_copy(3).start()
    leaf_copy.wait()
    tree_copy.wait()
    tiles = a_buf.shape[1] // lanes
    for t, dy in enumerate(far_first):
        a_copy(t).wait()
        y = (y0 + dy) % 4
        base = pl.multiple_of(y * step_rows, step_rows)
        for k in range(group):
            mine = column_of(leaf_ref[pl.ds(i * cols_n + y * group + k, 1), :]).astype(BF16)
            rows = pl.ds(pl.multiple_of(base + k * lanes, lanes), lanes)
            for c in range(tiles):
                theirs = leaf_ref[pl.ds(j * rows_n + c, 1), :].astype(BF16)
                block = a_buf[rows, c * lanes : (c + 1) * lanes]
                a_buf[rows, c * lanes : (c + 1) * lanes] = jnp.where(mine == theirs, jnp.zeros_like(block), block)
        if t == 0:
            right_copy.wait()
        forward = mm(a_buf[pl.ds(base, step_rows), :], right_buf[...]).astype(BF16)
        fs[pl.ds(y * group, group)] = forward.reshape(group, lanes, forward.shape[1])
        if t == 0:
            pl.semaphore_wait(barrier, cols_n + rows_n - 2)
        for dz in far_first:
            if (dy, dz) != (0, 0):
                peer = y * group + (z0 + dz) % group
                remote(fs.at[peer], fr.at[j], fs_sem.at[peer], fr_sem.at[j], {"col": peer}).start()
        if t == 0:
            left_copy.wait()
        part = mm(left_buf[pl.ds(base, step_rows), :], a_buf[pl.ds(base, step_rows), :], ATB)
        if t == 0:
            back[...] = part
        elif t < 3:
            back[...] += part
        else:
            part += back[...]
            for k in range(rows_n):
                bs[k % 2, k // 2] = part[:, k * lanes : (k + 1) * lanes]
    other = 1 - core
    chips = rows_n // 2

    def pair(k):
        x = (x0 + 1 + k) % chips
        return x, remote(bs.at[other, x], bp.at[x], ps_sem.at[x], pr_sem.at[x], {"row": x0 * 2 + other})

    def pair_start(k, carry):
        pair(k)[1].start()
        return carry

    lax.fori_loop(0, chips, pair_start, 0)

    def along(x):
        return remote(bsum.at[x], br.at[x0], bs_sem.at[x], br_sem.at[x0], {"row": x * 2 + core})

    def pair_end(k, carry):
        x, copy = pair(k)
        copy.wait()
        bsum[pl.ds(x, 1)] = bs[core, pl.ds(x, 1)] + bp[pl.ds(x, 1)]

        @pl.when(x != x0)
        def _():
            along(x).start()

        return carry

    lax.fori_loop(0, chips, pair_end, 0)

    tree = tree_ref[...]
    slots = out.shape[1]
    slot = iota((slots, lanes), 0)
    row_bits, col_bits = rows_n.bit_length() - 1, cols_n.bit_length() - 1
    f_place = (((slot >> 1) & (rows_n - 1)) << col_bits) + (slot >> (1 + row_bits))
    forward_map = spread_matrix(leaf_ref[pl.ds(i * cols_n + j, 1), :], tree, f_place, slot & 1)
    backward_map = spread_matrix(leaf_ref[pl.ds(j * rows_n + i, 1), :], tree, slot >> 1, slot & 1)

    def along_end(k, carry):
        x = (x0 + 1 + k) % chips
        along(x).wait_send()
        remote(bsum.at[x], br.at[x], bs_sem.at[x], br_sem.at[x], {"row": x * 2 + core}).wait_recv()
        return carry

    lax.fori_loop(0, chips - 1, along_end, 0)
    br[pl.ds(x0, 1)] = bsum[pl.ds(x0, 1)]
    sample_back = jnp.sum(br[...], axis=0).astype(BF16)
    width = out.shape[2]

    def rows_exchange(src, dst, send_sem, recv_sem):
        def start(k, carry):
            peer = (i + k) % rows_n
            remote(src.at[peer], dst.at[i], send_sem.at[peer], recv_sem.at[i], {"row": peer}).start()
            return carry

        def end(k, carry):
            peer = (i + k) % rows_n
            remote(src.at[peer], dst.at[peer], send_sem.at[peer], recv_sem.at[peer], {"row": peer}).wait()
            return carry

        return start, end

    def cols_exchange(src, dst, send_sem, recv_sem):
        def start(k, carry):
            peer = (j + k) % cols_n
            remote(src.at[peer], dst.at[j], send_sem.at[peer], recv_sem.at[j], {"col": peer}).start()
            return carry

        def end(k, carry):
            peer = (j + k) % cols_n
            remote(src.at[peer], dst.at[peer], send_sem.at[peer], recv_sem.at[peer], {"col": peer}).wait()
            return carry

        return start, end

    b1_start, b1_end = rows_exchange(b1s, b1r, b1s_sem, b1r_sem)
    f1_start, f1_end = cols_exchange(f1s, f1r, f1s_sem, f1r_sem)

    def back_part(col):
        return out.at[1, pl.ds(pl.multiple_of(col * 2 * rows_n, 2 * rows_n), 2 * rows_n)]

    def forward_part(row):
        return out.at[0, pl.ds(pl.multiple_of(row * 2 * cols_n, 2 * cols_n), 2 * cols_n)]

    def b2_start(k, carry):
        peer = (j + k) % cols_n
        remote(b2s.at[peer], back_part(j), b2s_sem.at[peer], b2r_sem.at[j], {"col": peer}).start()
        return carry

    def b2_end(k, carry):
        peer = (j + k) % cols_n
        remote(b2s.at[peer], back_part(peer), b2s_sem.at[peer], b2r_sem.at[peer], {"col": peer}).wait()
        return carry

    def f2_start(k, carry):
        peer = (i + k) % rows_n
        remote(f2s.at[peer], forward_part(i), f2s_sem.at[peer], f2r_sem.at[i], {"row": peer}).start()
        return carry

    def f2_end(k, carry):
        peer = (i + k) % rows_n
        remote(f2s.at[peer], forward_part(peer), f2s_sem.at[peer], f2r_sem.at[peer], {"row": peer}).wait()
        return carry

    b1s[...] = mm(backward_map, sample_back, ABT).astype(BF16).reshape(b1s.shape)
    lax.fori_loop(1, rows_n, b1_start, 0)
    b1r[pl.ds(i, 1)] = b1s[pl.ds(i, 1)]

    acc[...] = fs[pl.ds(j, 1)][0].astype(F32)
    near_first = sorted(
        ((dy, dz) for dy in range(4) for dz in range(4) if (dy, dz) != (0, 0)),
        key=lambda d: min(d[0], 4 - d[0]) + min(d[1], 4 - d[1]),
    )
    for dy, dz in near_first:
        peer = ((y0 + dy) % 4) * group + (z0 + dz) % group
        remote(fs.at[peer], fr.at[peer], fs_sem.at[peer], fr_sem.at[peer], {"col": peer}).wait()
        acc[...] += fr[pl.ds(peer, 1)][0].astype(F32)
    f1s[...] = mm(forward_map, acc[...].astype(BF16)).astype(BF16).reshape(f1s.shape)
    lax.fori_loop(1, cols_n, f1_start, 0)
    f1r[pl.ds(j, 1)] = f1s[pl.ds(j, 1)]

    slot = iota((slots, slots), 0)
    source = iota((slots, slots), 1)
    row_col = (((slot >> 1) & (cols_n - 1)) << (1 + row_bits)) + ((slot >> (1 + col_bits)) << 1) + (slot & 1)
    col_row = (((slot >> 1) & (rows_n - 1)) << (1 + col_bits)) + ((slot >> (1 + row_bits)) << 1) + (slot & 1)
    to_rows, to_cols = one_hot(source == row_col), one_hot(source == col_row)

    lax.fori_loop(1, rows_n, b1_end, 0)
    b2s[...] = mm(to_cols, b1r[...].reshape(slots, width)).astype(BF16).reshape(b2s.shape)
    lax.fori_loop(1, cols_n, b2_start, 0)
    back_own = pltpu.make_async_copy(b2s.at[j], back_part(j), in_sem.at[4])
    back_own.start()

    lax.fori_loop(1, cols_n, f1_end, 0)
    f2s[...] = mm(to_rows, f1r[...].reshape(slots, width)).astype(BF16).reshape(f2s.shape)
    lax.fori_loop(1, rows_n, f2_start, 0)
    forward_own = pltpu.make_async_copy(f2s.at[i], forward_part(i), in_sem.at[5])
    forward_own.start()

    back_own.wait()
    forward_own.wait()
    lax.fori_loop(1, cols_n, b2_end, 0)
    lax.fori_loop(1, rows_n, f2_end, 0)


def sample_call(front_block, probe_right, probe_left, leaves, tree, rows_n, cols_n):
    tile_rows, tile_cols = front_block.shape
    samples = probe_right.shape[1]
    lanes = leaves.shape[1]
    slots = 2 * rows_n * cols_n
    chips = rows_n // 2
    hbm = pl.BlockSpec(memory_space=pltpu.HBM)
    out = jax.ShapeDtypeStruct((2, slots, samples), BF16)
    by_col = pltpu.VMEM((cols_n, 2 * rows_n, samples), BF16)
    by_row = pltpu.VMEM((rows_n, 2 * cols_n, samples), BF16)
    dma = pltpu.SemaphoreType.DMA
    return pl.pallas_call(
        functools.partial(sample_kernel, rows_n, cols_n),
        out_shape=out,
        in_specs=[hbm] * 5,
        out_specs=pl.BlockSpec(memory_space=pl.ANY),
        scratch_shapes=[
            pltpu.VMEM(leaves.shape, jnp.int32),
            pltpu.VMEM(tree.shape, jnp.int32),
            pltpu.VMEM((tile_rows, tile_cols), BF16),
            pltpu.VMEM((tile_cols, samples), BF16),
            pltpu.VMEM((tile_rows, samples), BF16),
            pltpu.VMEM((cols_n, lanes, samples), BF16),
            pltpu.VMEM((cols_n, lanes, samples), BF16),
            pltpu.VMEM((samples, tile_cols), F32),
            pltpu.VMEM((2, chips, samples, lanes), F32),
            pltpu.VMEM((chips, samples, lanes), F32),
            pltpu.VMEM((chips, samples, lanes), F32),
            pltpu.VMEM((chips, samples, lanes), F32),
            by_col, by_col, by_row, by_row, by_row, by_col,
            pltpu.VMEM((lanes, samples), F32),
            dma((8,)),
            dma((cols_n,)), dma((cols_n,)),
            dma((chips,)), dma((chips,)), dma((chips,)), dma((chips,)),
            dma((cols_n,)), dma((cols_n,)), dma((rows_n,)), dma((rows_n,)),
            dma((rows_n,)), dma((rows_n,)), dma((cols_n,)), dma((cols_n,)),
        ],
        compiler_params=pltpu.CompilerParams(collective_id=0, has_side_effects=True, vmem_limit_bytes=67043328),
    )(front_block, probe_right, probe_left, leaves, tree)


def per_device(front_block, probe_right, probe_left, row_leaf, tree_leaf):
    rows_n, cols_n = lax.axis_size("row"), lax.axis_size("col")
    devices = rows_n * cols_n
    leaves = row_leaf.reshape(devices, row_leaf.shape[0] // devices)
    routed = sample_call(front_block, probe_right, probe_left, leaves, tree_leaf.reshape(1, devices), rows_n, cols_n)
    coupling, sent = dense_call(leaf_kernel, (F32, BF16), 1, routed)
    (merged,) = dense_call(merge_kernel, (F32,), 2, coupling, gather_call(sent))
    return (coupling[None], merged[None])


def solution(mesh):
    return jax.shard_map(
        per_device,
        mesh=mesh,
        in_specs=(P("row", "col"), P("col", None), P("row", None), P(), P()),
        out_specs=(P(("row", "col"), None, None), P(("row", "col"), None, None)),
        check_vma=False,
    )
```

```python
import functools

import jax
import jax.numpy as jnp
from jax import lax
from jax.experimental import pallas as pl
from jax.experimental.pallas import tpu as pltpu
from jax.sharding import PartitionSpec as P

eps = 1e-05
F32, BF16 = jnp.float32, jnp.bfloat16
AB = (((1,), (0,)), ((), ()))
ABT = (((1,), (1,)), ((), ()))
ATB = (((0,), (0,)), ((), ()))


def split(value):
    high = value.astype(BF16)
    return high, (value - high.astype(F32)).astype(BF16)


def mm(left, right, dims=AB):
    return lax.dot_general(left, right, dims, preferred_element_type=F32)


def mm3(left, right, dims=AB):
    return mm(left[0], right[0], dims) + (mm(left[0], right[1], dims) + mm(left[1], right[0], dims))


def whiten(problems, b_ref, x_ref, g_ref):
    width = problems[0][0].shape[0]
    row = lax.broadcasted_iota(jnp.int32, (width, width), 0)
    col = lax.broadcasted_iota(jnp.int32, (width, width), 1)
    below, diag = row > col, row == col

    def half(value):
        return jnp.where(below, value, jnp.where(diag, 0.5 * value, 0.0))

    def factor(value):
        return jnp.where(below, -value, jnp.where(diag, 1.5 - 0.5 * value, 0.0)).astype(BF16)

    def advance(b, t, growth):
        b = mm(mm(t, b.astype(BF16)).astype(BF16), t, ABT) * growth
        return b, factor(b)

    def error(x, n):
        y_high, y_low = split(mm(x, g_ref[n, 0]) + mm(x, g_ref[n, 1]))
        return half(mm(y_high, x, ABT) + mm(y_low, x, ABT) - diag.astype(F32))

    rhs, worst, states = [], None, []
    for n, (gram, squares, cross) in enumerate(problems):
        ridge = squares / width + eps
        inv_root = lax.rsqrt(ridge)
        unit = gram * (inv_root * inv_root) + diag.astype(F32)
        g_ref[n, 0], g_ref[n, 1] = split(unit)
        rhs.append(split(cross * inv_root))
        high = unit.astype(BF16)
        square = mm(high, high)
        fourth = total(square * square)
        worst = fourth if worst is None else jnp.maximum(worst, fourth)
        scale = 1.9 * lax.rsqrt(jnp.sqrt(fourth))
        b = unit * scale
        t = factor(b)
        states.append((b, t, t.astype(F32) * jnp.sqrt(scale * (1.3 * 1.2))))
    worst = jnp.sum(worst)
    steps = jnp.int32(3)
    for bound in (16.0, 24.0, 45.0, 100.0, 180.0):
        steps = steps + (worst > bound**4).astype(jnp.int32)
    extra = (worst > 48.0**4).astype(jnp.int32)

    for growth in (1.3, 1.2):
        states = [(*advance(b, t, growth), x) for b, t, x in states]
        states = [(b, t, mm(t, x.astype(BF16))) for b, t, x in states]
    for n, (b, t, x) in enumerate(states):
        b_ref[n] = b
        x_ref[n] = x

    def more(_, carry):
        for n in range(len(problems)):
            b, t = advance(b_ref[n], factor(b_ref[n]), 1.0)
            b_ref[n], x_ref[n] = b, mm(t, x_ref[n].astype(BF16))
        return carry

    def fix(_, carry):
        for n in range(len(problems)):
            x = x_ref[n].astype(BF16)
            x_ref[n] = x.astype(F32) - mm(error(x, n).astype(BF16), x)
        return carry

    lax.fori_loop(3, steps, more, 0)
    lax.fori_loop(0, extra, fix, 0)
    outs = []
    for n in range(len(problems)):
        x = x_ref[n].astype(BF16)
        z = mm(x, rhs[n][0]) + mm(x, rhs[n][1])
        outs.append(z - mm(error(x, n).astype(BF16), z.astype(BF16)))
    return outs


def total(value):
    return jnp.sum(jnp.sum(value, axis=1, keepdims=True), axis=0, keepdims=True)


def leaf_kernel(rows_ref, out_ref, send_ref, *refs):
    s, u = rows_ref[0], rows_ref[1]
    wide = s.astype(F32)
    s_t = s.T
    (out,) = whiten([(mm(s_t, s), total(wide * wide), mm(s_t, u))], *refs)
    out_ref[...] = out
    send_ref[...] = out.astype(BF16)


def product(left, right):
    out = mm(left[0], right[0])
    if left[1] is not None:
        out += mm(left[1], right[0])
    if right[1] is not None:
        out += mm(left[0], right[1])
    return out


def merge_parts(p, q):
    p_t, q_t = (tuple(None if part is None else part.T for part in node) for node in (p, q))
    squares = 0.0
    for high, low in (p, q):
        wide = high.astype(F32) if low is None else high.astype(F32) + low.astype(F32)
        squares += total(wide * wide)
    return product(p_t, p) + product(q_t, q), squares, product(p_t, q) + product(q_t, p)


def merge_kernel(p_ref, q_ref, out_ref, *refs):
    near, far = whiten(
        [merge_parts((p_ref[...], None), (q_ref[0], None)), merge_parts((q_ref[1], None), (q_ref[2], None))], *refs
    )
    (out_ref[...],) = whiten([merge_parts(split(near), split(far))], *refs)


def dense_call(kernel, out_shapes, problems, *args):
    width = args[0].shape[-1]
    whole = pl.BlockSpec(memory_space=pltpu.VMEM)
    return pl.pallas_call(
        kernel,
        out_shape=tuple(jax.ShapeDtypeStruct((width, width), dtype) for dtype in out_shapes),
        in_specs=[whole] * len(args),
        out_specs=(whole,) * len(out_shapes),
        scratch_shapes=[
            pltpu.VMEM((problems, width, width), F32),
            pltpu.VMEM((problems, width, width), F32),
            pltpu.VMEM((problems, 2, width, width), BF16),
        ],
        compiler_params=pltpu.CompilerParams(vmem_limit_bytes=67043328),
    )(*args)


def gather_kernel(sent, out, send_sem, recv_sem):
    j = lax.axis_index("col")
    z = j % 4
    peers = [j - z + near for near in (z + 1 - 2 * (z % 2), (z + 2) % 4, 3 - z)]
    mesh_id = pl.DeviceIdType.MESH
    barrier = pltpu.get_barrier_semaphore()
    for peer in peers:
        pl.semaphore_signal(barrier, inc=1, device_id={"col": peer}, device_id_type=mesh_id)
    pl.semaphore_wait(barrier, 3)
    copies = [
        pltpu.make_async_remote_copy(
            src_ref=sent, dst_ref=out.at[n], send_sem=send_sem.at[n], recv_sem=recv_sem.at[n],
            device_id={"col": peer}, device_id_type=mesh_id,
        )
        for n, peer in enumerate(peers)
    ]
    for n in (1, 0, 2):
        copies[n].start()
    for copy in copies:
        copy.wait()


def gather_call(sent):
    anywhere = pl.BlockSpec(memory_space=pl.ANY)
    return pl.pallas_call(
        gather_kernel,
        out_shape=jax.ShapeDtypeStruct((3, *sent.shape), sent.dtype),
        in_specs=[anywhere],
        out_specs=anywhere,
        scratch_shapes=[pltpu.SemaphoreType.DMA((3,)), pltpu.SemaphoreType.DMA((3,))],
        compiler_params=pltpu.CompilerParams(collective_id=1, has_side_effects=True, vmem_limit_bytes=67043328),
    )(sent)


def iota(shape, axis):
    return lax.broadcasted_iota(jnp.int32, shape, axis)


def one_hot(condition):
    return jnp.where(condition, 1.0, 0.0).astype(BF16)


def column_of(row):
    n = row.shape[1]
    eye = one_hot(iota((n, n), 0) == iota((n, n), 1))
    return mm(eye, jnp.broadcast_to(row, (n, n)).astype(BF16), ABT)


def spread_matrix(leaf_row, tree_row, place_of_slot, slot_rank):
    n = leaf_row.shape[1]
    slots = place_of_slot.shape[0]
    here = leaf_row.astype(F32)
    twin = jnp.where((column_of(leaf_row) == here) & (iota((n, n), 0) < iota((n, n), 1)), 1.0, 0.0)
    rank = jnp.sum(twin, axis=0, keepdims=True)
    pick = one_hot(place_of_slot == iota((slots, n), 1))
    named = mm(pick, jnp.broadcast_to(tree_row, (n, n)).astype(BF16), ABT)
    return one_hot((named == here) & (slot_rank.astype(F32) == rank))


def sample_kernel(
    rows_n, cols_n, a_hbm, right_hbm, left_hbm, leaf_hbm, tree_hbm, out,
    leaf_ref, tree_ref, a_buf, right_buf, left_buf, fs, fr, back, bs, bp, bsum, br,
    f1s, f1r, f2s, b1s, b1r, b2s, acc,
    in_sem, fs_sem, fr_sem, ps_sem, pr_sem, bs_sem, br_sem,
    f1s_sem, f1r_sem, f2s_sem, f2r_sem, b1s_sem, b1r_sem, b2s_sem, b2r_sem,
):
    i, j = lax.axis_index("row"), lax.axis_index("col")
    lanes = fs.shape[1]
    group = cols_n // 4
    step_rows = group * lanes
    y0, z0 = j // group, j % group
    far_first = (2, 1, 3, 0)
    x0, core = i // 2, i % 2
    mesh_id = pl.DeviceIdType.MESH

    def remote(src, dst, send_sem, recv_sem, device):
        return pltpu.make_async_remote_copy(
            src_ref=src, dst_ref=dst, send_sem=send_sem, recv_sem=recv_sem, device_id=device, device_id_type=mesh_id
        )

    barrier = pltpu.get_barrier_semaphore()

    def greet_col(k, _):
        pl.semaphore_signal(barrier, inc=1, device_id={"col": (j + k) % cols_n}, device_id_type=mesh_id)
        return _

    def greet_row(k, _):
        pl.semaphore_signal(barrier, inc=1, device_id={"row": (i + k) % rows_n}, device_id_type=mesh_id)
        return _

    lax.fori_loop(1, cols_n, greet_col, 0)
    lax.fori_loop(1, rows_n, greet_row, 0)

    right_copy = pltpu.make_async_copy(right_hbm, right_buf, in_sem.at[4])
    left_copy = pltpu.make_async_copy(left_hbm, left_buf, in_sem.at[5])
    leaf_copy = pltpu.make_async_copy(leaf_hbm, leaf_ref, in_sem.at[6])
    tree_copy = pltpu.make_async_copy(tree_hbm, tree_ref, in_sem.at[7])

    def rows_at(t):
        return pl.ds(pl.multiple_of(((y0 + far_first[t]) % 4) * step_rows, step_rows), step_rows)

    def a_copy(t):
        return pltpu.make_async_copy(a_hbm.at[rows_at(t)], a_buf.at[rows_at(t)], in_sem.at[t])

    leaf_copy.start()
    tree_copy.start()
    a_copy(0).start()
    right_copy.start()
    a_copy(1).start()
    left_copy.start()
    a_copy(2).start()
    a_copy(3).start()
    leaf_copy.wait()
    tree_copy.wait()
    tiles = a_buf.shape[1] // lanes
    for t, dy in enumerate(far_first):
        a_copy(t).wait()
        y = (y0 + dy) % 4
        base = pl.multiple_of(y * step_rows, step_rows)
        for k in range(group):
            mine = column_of(leaf_ref[pl.ds(i * cols_n + y * group + k, 1), :]).astype(BF16)
            rows = pl.ds(pl.multiple_of(base + k * lanes, lanes), lanes)
            for c in range(tiles):
                theirs = leaf_ref[pl.ds(j * rows_n + c, 1), :].astype(BF16)
                block = a_buf[rows, c * lanes : (c + 1) * lanes]
                a_buf[rows, c * lanes : (c + 1) * lanes] = jnp.where(mine == theirs, jnp.zeros_like(block), block)
        if t == 0:
            right_copy.wait()
        forward = mm(a_buf[pl.ds(base, step_rows), :], right_buf[...]).astype(BF16)
        fs[pl.ds(y * group, group)] = forward.reshape(group, lanes, forward.shape[1])
        if t == 0:
            pl.semaphore_wait(barrier, cols_n + rows_n - 2)
        for dz in far_first:
            if (dy, dz) != (0, 0):
                peer = y * group + (z0 + dz) % group
                remote(fs.at[peer], fr.at[j], fs_sem.at[peer], fr_sem.at[j], {"col": peer}).start()
        if t == 0:
            left_copy.wait()
        part = mm(left_buf[pl.ds(base, step_rows), :], a_buf[pl.ds(base, step_rows), :], ATB)
        if t == 0:
            back[...] = part
        elif t < 3:
            back[...] += part
        else:
            part += back[...]
            for k in range(rows_n):
                bs[k % 2, k // 2] = part[:, k * lanes : (k + 1) * lanes]
    other = 1 - core
    chips = rows_n // 2

    def pair(k):
        x = (x0 + 1 + k) % chips
        return x, remote(bs.at[other, x], bp.at[x], ps_sem.at[x], pr_sem.at[x], {"row": x0 * 2 + other})

    def pair_start(k, carry):
        pair(k)[1].start()
        return carry

    lax.fori_loop(0, chips, pair_start, 0)

    def along(x):
        return remote(bsum.at[x], br.at[x0], bs_sem.at[x], br_sem.at[x0], {"row": x * 2 + core})

    def pair_end(k, carry):
        x, copy = pair(k)
        copy.wait()
        bsum[pl.ds(x, 1)] = bs[core, pl.ds(x, 1)] + bp[pl.ds(x, 1)]

        @pl.when(x != x0)
        def _():
            along(x).start()

        return carry

    lax.fori_loop(0, chips, pair_end, 0)

    tree = tree_ref[...]
    slots = out.shape[1]
    slot = iota((slots, lanes), 0)
    row_bits, col_bits = rows_n.bit_length() - 1, cols_n.bit_length() - 1
    f_place = (((slot >> 1) & (rows_n - 1)) << col_bits) + (slot >> (1 + row_bits))
    forward_map = spread_matrix(leaf_ref[pl.ds(i * cols_n + j, 1), :], tree, f_place, slot & 1)
    backward_map = spread_matrix(leaf_ref[pl.ds(j * rows_n + i, 1), :], tree, slot >> 1, slot & 1)

    def along_end(k, carry):
        x = (x0 + 1 + k) % chips
        along(x).wait_send()
        remote(bsum.at[x], br.at[x], bs_sem.at[x], br_sem.at[x], {"row": x * 2 + core}).wait_recv()
        return carry

    lax.fori_loop(0, chips - 1, along_end, 0)
    br[pl.ds(x0, 1)] = bsum[pl.ds(x0, 1)]
    sample_back = jnp.sum(br[...], axis=0).astype(BF16)
    width = out.shape[2]

    def rows_exchange(src, dst, send_sem, recv_sem):
        def start(k, carry):
            peer = (i + k) % rows_n
            remote(src.at[peer], dst.at[i], send_sem.at[peer], recv_sem.at[i], {"row": peer}).start()
            return carry

        def end(k, carry):
            peer = (i + k) % rows_n
            remote(src.at[peer], dst.at[peer], send_sem.at[peer], recv_sem.at[peer], {"row": peer}).wait()
            return carry

        return start, end

    def cols_exchange(src, dst, send_sem, recv_sem):
        def start(k, carry):
            peer = (j + k) % cols_n
            remote(src.at[peer], dst.at[j], send_sem.at[peer], recv_sem.at[j], {"col": peer}).start()
            return carry

        def end(k, carry):
            peer = (j + k) % cols_n
            remote(src.at[peer], dst.at[peer], send_sem.at[peer], recv_sem.at[peer], {"col": peer}).wait()
            return carry

        return start, end

    b1_start, b1_end = rows_exchange(b1s, b1r, b1s_sem, b1r_sem)
    f1_start, f1_end = cols_exchange(f1s, f1r, f1s_sem, f1r_sem)

    def back_part(col):
        return out.at[1, pl.ds(pl.multiple_of(col * 2 * rows_n, 2 * rows_n), 2 * rows_n)]

    def forward_part(row):
        return out.at[0, pl.ds(pl.multiple_of(row * 2 * cols_n, 2 * cols_n), 2 * cols_n)]

    def b2_start(k, carry):
        peer = (j + k) % cols_n
        remote(b2s.at[peer], back_part(j), b2s_sem.at[peer], b2r_sem.at[j], {"col": peer}).start()
        return carry

    def b2_end(k, carry):
        peer = (j + k) % cols_n
        remote(b2s.at[peer], back_part(peer), b2s_sem.at[peer], b2r_sem.at[peer], {"col": peer}).wait()
        return carry

    def f2_start(k, carry):
        peer = (i + k) % rows_n
        remote(f2s.at[peer], forward_part(i), f2s_sem.at[peer], f2r_sem.at[i], {"row": peer}).start()
        return carry

    def f2_end(k, carry):
        peer = (i + k) % rows_n
        remote(f2s.at[peer], forward_part(peer), f2s_sem.at[peer], f2r_sem.at[peer], {"row": peer}).wait()
        return carry

    b1s[...] = mm(backward_map, sample_back, ABT).astype(BF16).reshape(b1s.shape)
    lax.fori_loop(1, rows_n, b1_start, 0)
    b1r[pl.ds(i, 1)] = b1s[pl.ds(i, 1)]

    acc[...] = fs[pl.ds(j, 1)][0].astype(F32)
    near_first = sorted(
        ((dy, dz) for dy in range(4) for dz in range(4) if (dy, dz) != (0, 0)),
        key=lambda d: min(d[0], 4 - d[0]) + min(d[1], 4 - d[1]),
    )
    for dy, dz in near_first:
        peer = ((y0 + dy) % 4) * group + (z0 + dz) % group
        remote(fs.at[peer], fr.at[peer], fs_sem.at[peer], fr_sem.at[peer], {"col": peer}).wait()
        acc[...] += fr[pl.ds(peer, 1)][0].astype(F32)
    f1s[...] = mm(forward_map, acc[...].astype(BF16)).astype(BF16).reshape(f1s.shape)
    lax.fori_loop(1, cols_n, f1_start, 0)
    f1r[pl.ds(j, 1)] = f1s[pl.ds(j, 1)]

    slot = iota((slots, slots), 0)
    source = iota((slots, slots), 1)
    row_col = (((slot >> 1) & (cols_n - 1)) << (1 + row_bits)) + ((slot >> (1 + col_bits)) << 1) + (slot & 1)
    col_row = (((slot >> 1) & (rows_n - 1)) << (1 + col_bits)) + ((slot >> (1 + row_bits)) << 1) + (slot & 1)
    to_rows, to_cols = one_hot(source == row_col), one_hot(source == col_row)

    lax.fori_loop(1, rows_n, b1_end, 0)
    b2s[...] = mm(to_cols, b1r[...].reshape(slots, width)).astype(BF16).reshape(b2s.shape)
    lax.fori_loop(1, cols_n, b2_start, 0)
    back_own = pltpu.make_async_copy(b2s.at[j], back_part(j), in_sem.at[4])
    back_own.start()

    lax.fori_loop(1, cols_n, f1_end, 0)
    f2s[...] = mm(to_rows, f1r[...].reshape(slots, width)).astype(BF16).reshape(f2s.shape)
    lax.fori_loop(1, rows_n, f2_start, 0)
    forward_own = pltpu.make_async_copy(f2s.at[i], forward_part(i), in_sem.at[5])
    forward_own.start()

    back_own.wait()
    forward_own.wait()
    lax.fori_loop(1, cols_n, b2_end, 0)
    lax.fori_loop(1, rows_n, f2_end, 0)


def sample_call(front_block, probe_right, probe_left, leaves, tree, rows_n, cols_n):
    tile_rows, tile_cols = front_block.shape
    samples = probe_right.shape[1]
    lanes = leaves.shape[1]
    slots = 2 * rows_n * cols_n
    chips = rows_n // 2
    hbm = pl.BlockSpec(memory_space=pltpu.HBM)
    out = jax.ShapeDtypeStruct((2, slots, samples), BF16)
    by_col = pltpu.VMEM((cols_n, 2 * rows_n, samples), BF16)
    by_row = pltpu.VMEM((rows_n, 2 * cols_n, samples), BF16)
    dma = pltpu.SemaphoreType.DMA
    return pl.pallas_call(
        functools.partial(sample_kernel, rows_n, cols_n),
        out_shape=out,
        in_specs=[hbm] * 5,
        out_specs=pl.BlockSpec(memory_space=pl.ANY),
        scratch_shapes=[
            pltpu.VMEM(leaves.shape, jnp.int32),
            pltpu.VMEM(tree.shape, jnp.int32),
            pltpu.VMEM((tile_rows, tile_cols), BF16),
            pltpu.VMEM((tile_cols, samples), BF16),
            pltpu.VMEM((tile_rows, samples), BF16),
            pltpu.VMEM((cols_n, lanes, samples), BF16),
            pltpu.VMEM((cols_n, lanes, samples), BF16),
            pltpu.VMEM((samples, tile_cols), F32),
            pltpu.VMEM((2, chips, samples, lanes), F32),
            pltpu.VMEM((chips, samples, lanes), F32),
            pltpu.VMEM((chips, samples, lanes), F32),
            pltpu.VMEM((chips, samples, lanes), F32),
            by_col, by_col, by_row, by_row, by_row, by_col,
            pltpu.VMEM((lanes, samples), F32),
            dma((8,)),
            dma((cols_n,)), dma((cols_n,)),
            dma((chips,)), dma((chips,)), dma((chips,)), dma((chips,)),
            dma((cols_n,)), dma((cols_n,)), dma((rows_n,)), dma((rows_n,)),
            dma((rows_n,)), dma((rows_n,)), dma((cols_n,)), dma((cols_n,)),
        ],
        compiler_params=pltpu.CompilerParams(collective_id=0, has_side_effects=True, vmem_limit_bytes=67043328),
    )(front_block, probe_right, probe_left, leaves, tree)


def per_device(front_block, probe_right, probe_left, row_leaf, tree_leaf):
    rows_n, cols_n = lax.axis_size("row"), lax.axis_size("col")
    devices = rows_n * cols_n
    leaves = row_leaf.reshape(devices, row_leaf.shape[0] // devices)
    routed = sample_call(front_block, probe_right, probe_left, leaves, tree_leaf.reshape(1, devices), rows_n, cols_n)
    coupling, sent = dense_call(leaf_kernel, (F32, BF16), 1, routed)
    (merged,) = dense_call(merge_kernel, (F32,), 2, sent, gather_call(sent))
    return (coupling[None], merged[None])


def solution(mesh):
    return jax.shard_map(
        per_device,
        mesh=mesh,
        in_specs=(P("row", "col"), P("col", None), P("row", None), P(), P()),
        out_specs=(P(("row", "col"), None, None), P(("row", "col"), None, None)),
        check_vma=False,
    )
```

```python
import functools

import jax
import jax.numpy as jnp
from jax import lax
from jax.experimental import pallas as pl
from jax.experimental.pallas import tpu as pltpu
from jax.sharding import PartitionSpec as P

eps = 1e-05
F32, BF16 = jnp.float32, jnp.bfloat16
AB = (((1,), (0,)), ((), ()))
ABT = (((1,), (1,)), ((), ()))
ATB = (((0,), (0,)), ((), ()))


def split(value):
    high = value.astype(BF16)
    return high, (value - high.astype(F32)).astype(BF16)


def mm(left, right, dims=AB):
    return lax.dot_general(left, right, dims, preferred_element_type=F32)


def mm3(left, right, dims=AB):
    return mm(left[0], right[0], dims) + (mm(left[0], right[1], dims) + mm(left[1], right[0], dims))


def whiten(problems, b_ref, x_ref, g_ref):
    width = problems[0][0].shape[0]
    row = lax.broadcasted_iota(jnp.int32, (width, width), 0)
    col = lax.broadcasted_iota(jnp.int32, (width, width), 1)
    below, diag = row > col, row == col

    def half(value):
        return jnp.where(below, value, jnp.where(diag, 0.5 * value, 0.0))

    def factor(value):
        return jnp.where(below, -value, jnp.where(diag, 1.5 - 0.5 * value, 0.0)).astype(BF16)

    def advance(b, t, growth):
        b = mm(mm(t, b.astype(BF16)).astype(BF16), t, ABT) * growth
        return b, factor(b)

    def error(x, n):
        y_high, y_low = split(mm(x, g_ref[n, 0]) + mm(x, g_ref[n, 1]))
        return half(mm(y_high, x, ABT) + mm(y_low, x, ABT) - diag.astype(F32))

    rhs, worst, states = [], None, []
    for n, (gram, squares, cross) in enumerate(problems):
        ridge = squares / width + eps
        inv_root = lax.rsqrt(ridge)
        unit = gram * (inv_root * inv_root) + diag.astype(F32)
        g_ref[n, 0], g_ref[n, 1] = split(unit)
        rhs.append(split(cross * inv_root))
        high = unit.astype(BF16)
        square = mm(high, high)
        fourth = total(square * square)
        worst = fourth if worst is None else jnp.maximum(worst, fourth)
        scale = 1.9 * lax.rsqrt(jnp.sqrt(fourth))
        b = unit * scale
        t = factor(b)
        states.append((b, t, t.astype(F32) * jnp.sqrt(scale * (1.3 * 1.2))))
    worst = jnp.sum(worst)
    steps = jnp.int32(3)
    for bound in (16.0, 24.0, 45.0, 100.0, 180.0):
        steps = steps + (worst > bound**4).astype(jnp.int32)
    extra = (worst > 48.0**4).astype(jnp.int32)

    for growth in (1.3, 1.2):
        states = [(*advance(b, t, growth), x) for b, t, x in states]
        states = [(b, t, mm(t, x.astype(BF16))) for b, t, x in states]
    for n, (b, t, x) in enumerate(states):
        b_ref[n] = b
        x_ref[n] = x

    def more(_, carry):
        for n in range(len(problems)):
            b, t = advance(b_ref[n], factor(b_ref[n]), 1.0)
            b_ref[n], x_ref[n] = b, mm(t, x_ref[n].astype(BF16))
        return carry

    def fix(_, carry):
        for n in range(len(problems)):
            x = x_ref[n].astype(BF16)
            x_ref[n] = x.astype(F32) - mm(error(x, n).astype(BF16), x)
        return carry

    lax.fori_loop(3, steps, more, 0)
    lax.fori_loop(0, extra, fix, 0)
    outs = []
    for n in range(len(problems)):
        x = x_ref[n].astype(BF16)
        z = mm(x, rhs[n][0]) + mm(x, rhs[n][1])
        outs.append(z - mm(error(x, n).astype(BF16), z.astype(BF16)))
    return outs


def total(value):
    return jnp.sum(jnp.sum(value, axis=1, keepdims=True), axis=0, keepdims=True)


def leaf_kernel(rows_ref, out_ref, send_ref, *refs):
    s, u = rows_ref[0], rows_ref[1]
    wide = s.astype(F32)
    s_t = s.T
    (out,) = whiten([(mm(s_t, s), total(wide * wide), mm(s_t, u))], *refs)
    out_ref[...] = out
    send_ref[...] = out.astype(BF16)


def product(left, right):
    out = mm(left[0], right[0])
    if left[1] is not None:
        out += mm(left[1], right[0])
    if right[1] is not None:
        out += mm(left[0], right[1])
    return out


def merge_parts(p, q):
    p_t, q_t = (tuple(None if part is None else part.T for part in node) for node in (p, q))
    squares = 0.0
    for high, low in (p, q):
        wide = high.astype(F32) if low is None else high.astype(F32) + low.astype(F32)
        squares += total(wide * wide)
    return product(p_t, p) + product(q_t, q), squares, product(p_t, q) + product(q_t, p)


def merge_kernel(p_ref, q_ref, out_ref, *refs):
    near, far = whiten(
        [merge_parts((p_ref[...], None), (q_ref[0], None)), merge_parts((q_ref[1], None), (q_ref[2], None))], *refs
    )
    (out_ref[...],) = whiten([merge_parts(split(near), split(far))], *refs)


def dense_call(kernel, out_shapes, problems, *args):
    width = args[0].shape[-1]
    whole = pl.BlockSpec(memory_space=pltpu.VMEM)
    return pl.pallas_call(
        kernel,
        out_shape=tuple(jax.ShapeDtypeStruct((width, width), dtype) for dtype in out_shapes),
        in_specs=[whole] * len(args),
        out_specs=(whole,) * len(out_shapes),
        scratch_shapes=[
            pltpu.VMEM((problems, width, width), F32),
            pltpu.VMEM((problems, width, width), F32),
            pltpu.VMEM((problems, 2, width, width), BF16),
        ],
        compiler_params=pltpu.CompilerParams(vmem_limit_bytes=67043328),
    )(*args)


def gather_kernel(sent, out, send_sem, recv_sem):
    j = lax.axis_index("col")
    z = j % 4
    peers = [j - z + near for near in (z + 1 - 2 * (z % 2), (z + 2) % 4, 3 - z)]
    mesh_id = pl.DeviceIdType.MESH
    barrier = pltpu.get_barrier_semaphore()
    for peer in peers:
        pl.semaphore_signal(barrier, inc=1, device_id={"col": peer}, device_id_type=mesh_id)
    pl.semaphore_wait(barrier, 3)
    copies = [
        pltpu.make_async_remote_copy(
            src_ref=sent, dst_ref=out.at[n], send_sem=send_sem.at[n], recv_sem=recv_sem.at[n],
            device_id={"col": peer}, device_id_type=mesh_id,
        )
        for n, peer in enumerate(peers)
    ]
    for n in (1, 0, 2):
        copies[n].start()
    for copy in copies:
        copy.wait()


def gather_call(sent):
    anywhere = pl.BlockSpec(memory_space=pl.ANY)
    return pl.pallas_call(
        gather_kernel,
        out_shape=jax.ShapeDtypeStruct((3, *sent.shape), sent.dtype),
        in_specs=[anywhere],
        out_specs=anywhere,
        scratch_shapes=[pltpu.SemaphoreType.DMA((3,)), pltpu.SemaphoreType.DMA((3,))],
        compiler_params=pltpu.CompilerParams(collective_id=1, has_side_effects=True, vmem_limit_bytes=67043328),
    )(sent)


def iota(shape, axis):
    return lax.broadcasted_iota(jnp.int32, shape, axis)


def one_hot(condition):
    return jnp.where(condition, 1.0, 0.0).astype(BF16)


def column_of(row):
    n = row.shape[1]
    eye = one_hot(iota((n, n), 0) == iota((n, n), 1))
    return mm(eye, jnp.broadcast_to(row, (n, n)).astype(BF16), ABT)


def spread_matrix(leaf_row, tree_row, place_of_slot, slot_rank):
    n = leaf_row.shape[1]
    slots = place_of_slot.shape[0]
    here = leaf_row.astype(F32)
    twin = jnp.where((column_of(leaf_row) == here) & (iota((n, n), 0) < iota((n, n), 1)), 1.0, 0.0)
    rank = jnp.sum(twin, axis=0, keepdims=True)
    pick = one_hot(place_of_slot == iota((slots, n), 1))
    named = mm(pick, jnp.broadcast_to(tree_row, (n, n)).astype(BF16), ABT)
    return one_hot((named == here) & (slot_rank.astype(F32) == rank))


def sample_kernel(
    rows_n, cols_n, a_hbm, right_hbm, left_hbm, leaf_hbm, tree_hbm, out,
    leaf_ref, tree_ref, a_buf, right_buf, left_buf, left_t, fs, fr, bs, bp, bsum, br,
    f1s, f1r, f2s, b1s, b1r, b2s, acc,
    in_sem, fs_sem, fr_sem, ps_sem, pr_sem, bs_sem, br_sem,
    f1s_sem, f1r_sem, f2s_sem, f2r_sem, b1s_sem, b1r_sem, b2s_sem, b2r_sem,
):
    i, j = lax.axis_index("row"), lax.axis_index("col")
    lanes = fs.shape[1]
    group = cols_n // 4
    step_rows = group * lanes
    y0, z0 = j // group, j % group
    far_first = (2, 1, 3, 0)
    x0, core = i // 2, i % 2
    mesh_id = pl.DeviceIdType.MESH

    def remote(src, dst, send_sem, recv_sem, device):
        return pltpu.make_async_remote_copy(
            src_ref=src, dst_ref=dst, send_sem=send_sem, recv_sem=recv_sem, device_id=device, device_id_type=mesh_id
        )

    barrier = pltpu.get_barrier_semaphore()

    def greet_col(k, _):
        pl.semaphore_signal(barrier, inc=1, device_id={"col": (j + k) % cols_n}, device_id_type=mesh_id)
        return _

    def greet_row(k, _):
        pl.semaphore_signal(barrier, inc=1, device_id={"row": (i + k) % rows_n}, device_id_type=mesh_id)
        return _

    lax.fori_loop(1, cols_n, greet_col, 0)
    lax.fori_loop(1, rows_n, greet_row, 0)

    right_copy = pltpu.make_async_copy(right_hbm, right_buf, in_sem.at[4])
    leaf_copy = pltpu.make_async_copy(leaf_hbm, leaf_ref, in_sem.at[6])
    tree_copy = pltpu.make_async_copy(tree_hbm, tree_ref, in_sem.at[7])

    def rows_at(t):
        return pl.ds(pl.multiple_of(((y0 + far_first[t]) % 4) * step_rows, step_rows), step_rows)

    def a_copy(t):
        return pltpu.make_async_copy(a_hbm.at[rows_at(t)], a_buf.at[pl.ds(t * step_rows, step_rows)], in_sem.at[t])

    def left_copy(t):
        return pltpu.make_async_copy(
            left_hbm.at[rows_at(t)], left_buf.at[pl.ds(t * step_rows, step_rows)], in_sem.at[8 + t]
        )

    leaf_copy.start()
    tree_copy.start()
    a_copy(0).start()
    right_copy.start()
    for t in range(1, 4):
        a_copy(t).start()
    for t in range(4):
        left_copy(t).start()
    tiles = a_buf.shape[1] // lanes

    def mask(t):
        y = (y0 + far_first[t]) % 4
        for k in range(group):
            mine = column_of(leaf_ref[pl.ds(i * cols_n + y * group + k, 1), :]).astype(BF16)
            rows = slice(t * step_rows + k * lanes, t * step_rows + (k + 1) * lanes)
            for c in range(tiles):
                theirs = leaf_ref[pl.ds(j * rows_n + c, 1), :].astype(BF16)
                block = a_buf[rows, c * lanes : (c + 1) * lanes]
                a_buf[rows, c * lanes : (c + 1) * lanes] = jnp.where(mine == theirs, jnp.zeros_like(block), block)

    def forward(t):
        y = (y0 + far_first[t]) % 4
        part = mm(a_buf[t * step_rows : (t + 1) * step_rows, :], right_buf[...]).astype(BF16)
        fs[pl.ds(y * group, group)] = part.reshape(group, lanes, part.shape[1])

    def turn(t):
        rows = slice(t * step_rows, (t + 1) * step_rows)
        left_t[:, rows] = left_buf[rows, :].T

    def distance(d):
        return min(d[0], 4 - d[0]) + min(d[1], 4 - d[1])

    near_first = sorted(((dy, dz) for dy in range(4) for dz in range(4) if (dy, dz) != (0, 0)), key=distance)

    leaf_copy.wait()
    tree_copy.wait()
    a_copy(0).wait()
    mask(0)
    right_copy.wait()
    a_copy(1).wait()
    mask(1)
    forward(0)
    a_copy(2).wait()
    left_copy(0).wait()
    left_copy(1).wait()
    mask(2)
    forward(1)
    turn(0)
    turn(1)
    a_copy(3).wait()
    left_copy(2).wait()
    left_copy(3).wait()
    mask(3)
    forward(2)
    turn(2)
    turn(3)
    forward(3)
    pl.semaphore_wait(barrier, cols_n + rows_n - 2)
    for dy, dz in reversed(near_first):
        peer = ((y0 + dy) % 4) * group + (z0 + dz) % group
        remote(fs.at[peer], fr.at[j], fs_sem.at[peer], fr_sem.at[j], {"col": peer}).start()

    other = 1 - core
    chips = rows_n // 2

    def pair(x):
        return remote(bs.at[other, x], bp.at[x], ps_sem.at[x], pr_sem.at[x], {"row": x0 * 2 + other})

    def along(x):
        return remote(bsum.at[x], br.at[x0], bs_sem.at[x], br_sem.at[x0], {"row": x * 2 + core})

    for dx in far_first:
        x = (x0 + dx) % chips
        part = mm(left_t[...], a_buf[:, pl.ds(pl.multiple_of(x * 2 * lanes, 2 * lanes), 2 * lanes)])
        bs[0, pl.ds(x, 1)] = part[None, :, :lanes]
        bs[1, pl.ds(x, 1)] = part[None, :, lanes:]
        pair(x).start()
    for dx in far_first:
        x = (x0 + dx) % chips
        pair(x).wait()
        bsum[pl.ds(x, 1)] = bs[core, pl.ds(x, 1)] + bp[pl.ds(x, 1)]
        if dx:
            along(x).start()

    tree = tree_ref[...]
    slots = out.shape[1]
    slot = iota((slots, lanes), 0)
    row_bits, col_bits = rows_n.bit_length() - 1, cols_n.bit_length() - 1
    f_place = (((slot >> 1) & (rows_n - 1)) << col_bits) + (slot >> (1 + row_bits))
    forward_map = spread_matrix(leaf_ref[pl.ds(i * cols_n + j, 1), :], tree, f_place, slot & 1)
    backward_map = spread_matrix(leaf_ref[pl.ds(j * rows_n + i, 1), :], tree, slot >> 1, slot & 1)

    def along_end(k, carry):
        x = (x0 + 1 + k) % chips
        along(x).wait_send()
        remote(bsum.at[x], br.at[x], bs_sem.at[x], br_sem.at[x], {"row": x * 2 + core}).wait_recv()
        return carry

    lax.fori_loop(0, chips - 1, along_end, 0)
    br[pl.ds(x0, 1)] = bsum[pl.ds(x0, 1)]
    sample_back = jnp.sum(br[...], axis=0).astype(BF16)
    width = out.shape[2]

    def rows_exchange(src, dst, send_sem, recv_sem):
        def start(k, carry):
            peer = (i + k) % rows_n
            remote(src.at[peer], dst.at[i], send_sem.at[peer], recv_sem.at[i], {"row": peer}).start()
            return carry

        def end(k, carry):
            peer = (i + k) % rows_n
            remote(src.at[peer], dst.at[peer], send_sem.at[peer], recv_sem.at[peer], {"row": peer}).wait()
            return carry

        return start, end

    def cols_exchange(src, dst, send_sem, recv_sem):
        def start(k, carry):
            peer = (j + k) % cols_n
            remote(src.at[peer], dst.at[j], send_sem.at[peer], recv_sem.at[j], {"col": peer}).start()
            return carry

        def end(k, carry):
            peer = (j + k) % cols_n
            remote(src.at[peer], dst.at[peer], send_sem.at[peer], recv_sem.at[peer], {"col": peer}).wait()
            return carry

        return start, end

    b1_start, b1_end = rows_exchange(b1s, b1r, b1s_sem, b1r_sem)
    f1_start, f1_end = cols_exchange(f1s, f1r, f1s_sem, f1r_sem)

    def back_part(col):
        return out.at[1, pl.ds(pl.multiple_of(col * 2 * rows_n, 2 * rows_n), 2 * rows_n)]

    def forward_part(row):
        return out.at[0, pl.ds(pl.multiple_of(row * 2 * cols_n, 2 * cols_n), 2 * cols_n)]

    def b2_start(k, carry):
        peer = (j + k) % cols_n
        remote(b2s.at[peer], back_part(j), b2s_sem.at[peer], b2r_sem.at[j], {"col": peer}).start()
        return carry

    def b2_end(k, carry):
        peer = (j + k) % cols_n
        remote(b2s.at[peer], back_part(peer), b2s_sem.at[peer], b2r_sem.at[peer], {"col": peer}).wait()
        return carry

    def f2_start(k, carry):
        peer = (i + k) % rows_n
        remote(f2s.at[peer], forward_part(i), f2s_sem.at[peer], f2r_sem.at[i], {"row": peer}).start()
        return carry

    def f2_end(k, carry):
        peer = (i + k) % rows_n
        remote(f2s.at[peer], forward_part(peer), f2s_sem.at[peer], f2r_sem.at[peer], {"row": peer}).wait()
        return carry

    b1s[...] = mm(backward_map, sample_back, ABT).astype(BF16).reshape(b1s.shape)
    lax.fori_loop(1, rows_n, b1_start, 0)
    b1r[pl.ds(i, 1)] = b1s[pl.ds(i, 1)]

    acc[...] = fs[pl.ds(j, 1)][0].astype(F32)
    for dy, dz in near_first:
        peer = ((y0 + dy) % 4) * group + (z0 + dz) % group
        remote(fs.at[peer], fr.at[peer], fs_sem.at[peer], fr_sem.at[peer], {"col": peer}).wait()
        acc[...] += fr[pl.ds(peer, 1)][0].astype(F32)
    f1s[...] = mm(forward_map, acc[...].astype(BF16)).astype(BF16).reshape(f1s.shape)
    lax.fori_loop(1, cols_n, f1_start, 0)
    f1r[pl.ds(j, 1)] = f1s[pl.ds(j, 1)]

    slot = iota((slots, slots), 0)
    source = iota((slots, slots), 1)
    row_col = (((slot >> 1) & (cols_n - 1)) << (1 + row_bits)) + ((slot >> (1 + col_bits)) << 1) + (slot & 1)
    col_row = (((slot >> 1) & (rows_n - 1)) << (1 + col_bits)) + ((slot >> (1 + row_bits)) << 1) + (slot & 1)
    to_rows, to_cols = one_hot(source == row_col), one_hot(source == col_row)

    lax.fori_loop(1, rows_n, b1_end, 0)
    b2s[...] = mm(to_cols, b1r[...].reshape(slots, width)).astype(BF16).reshape(b2s.shape)
    lax.fori_loop(1, cols_n, b2_start, 0)
    back_own = pltpu.make_async_copy(b2s.at[j], back_part(j), in_sem.at[4])
    back_own.start()

    lax.fori_loop(1, cols_n, f1_end, 0)
    f2s[...] = mm(to_rows, f1r[...].reshape(slots, width)).astype(BF16).reshape(f2s.shape)
    lax.fori_loop(1, rows_n, f2_start, 0)
    forward_own = pltpu.make_async_copy(f2s.at[i], forward_part(i), in_sem.at[5])
    forward_own.start()

    back_own.wait()
    forward_own.wait()
    lax.fori_loop(1, cols_n, b2_end, 0)
    lax.fori_loop(1, rows_n, f2_end, 0)


def sample_call(front_block, probe_right, probe_left, leaves, tree, rows_n, cols_n):
    tile_rows, tile_cols = front_block.shape
    samples = probe_right.shape[1]
    lanes = leaves.shape[1]
    slots = 2 * rows_n * cols_n
    chips = rows_n // 2
    hbm = pl.BlockSpec(memory_space=pltpu.HBM)
    out = jax.ShapeDtypeStruct((2, slots, samples), BF16)
    by_col = pltpu.VMEM((cols_n, 2 * rows_n, samples), BF16)
    by_row = pltpu.VMEM((rows_n, 2 * cols_n, samples), BF16)
    dma = pltpu.SemaphoreType.DMA
    return pl.pallas_call(
        functools.partial(sample_kernel, rows_n, cols_n),
        out_shape=out,
        in_specs=[hbm] * 5,
        out_specs=pl.BlockSpec(memory_space=pl.ANY),
        scratch_shapes=[
            pltpu.VMEM(leaves.shape, jnp.int32),
            pltpu.VMEM(tree.shape, jnp.int32),
            pltpu.VMEM((tile_rows, tile_cols), BF16),
            pltpu.VMEM((tile_cols, samples), BF16),
            pltpu.VMEM((tile_rows, samples), BF16),
            pltpu.VMEM((samples, tile_rows), BF16),
            pltpu.VMEM((cols_n, lanes, samples), BF16),
            pltpu.VMEM((cols_n, lanes, samples), BF16),
            pltpu.VMEM((2, chips, samples, lanes), F32),
            pltpu.VMEM((chips, samples, lanes), F32),
            pltpu.VMEM((chips, samples, lanes), F32),
            pltpu.VMEM((chips, samples, lanes), F32),
            by_col, by_col, by_row, by_row, by_row, by_col,
            pltpu.VMEM((lanes, samples), F32),
            dma((12,)),
            dma((cols_n,)), dma((cols_n,)),
            dma((chips,)), dma((chips,)), dma((chips,)), dma((chips,)),
            dma((cols_n,)), dma((cols_n,)), dma((rows_n,)), dma((rows_n,)),
            dma((rows_n,)), dma((rows_n,)), dma((cols_n,)), dma((cols_n,)),
        ],
        compiler_params=pltpu.CompilerParams(collective_id=0, has_side_effects=True, vmem_limit_bytes=67043328),
    )(front_block, probe_right, probe_left, leaves, tree)


def per_device(front_block, probe_right, probe_left, row_leaf, tree_leaf):
    rows_n, cols_n = lax.axis_size("row"), lax.axis_size("col")
    devices = rows_n * cols_n
    leaves = row_leaf.reshape(devices, row_leaf.shape[0] // devices)
    routed = sample_call(front_block, probe_right, probe_left, leaves, tree_leaf.reshape(1, devices), rows_n, cols_n)
    coupling, sent = dense_call(leaf_kernel, (F32, BF16), 1, routed)
    (merged,) = dense_call(merge_kernel, (F32,), 2, sent, gather_call(sent))
    return (coupling[None], merged[None])


def solution(mesh):
    return jax.shard_map(
        per_device,
        mesh=mesh,
        in_specs=(P("row", "col"), P("col", None), P("row", None), P(), P()),
        out_specs=(P(("row", "col"), None, None), P(("row", "col"), None, None)),
        check_vma=False,
    )
```

```python
import functools

import jax
import jax.numpy as jnp
from jax import lax
from jax.experimental import pallas as pl
from jax.experimental.pallas import tpu as pltpu
from jax.sharding import PartitionSpec as P

eps = 1e-05
F32, BF16 = jnp.float32, jnp.bfloat16
AB = (((1,), (0,)), ((), ()))
ABT = (((1,), (1,)), ((), ()))
ATB = (((0,), (0,)), ((), ()))


def split(value):
    high = value.astype(BF16)
    return high, (value - high.astype(F32)).astype(BF16)


def mm(left, right, dims=AB):
    return lax.dot_general(left, right, dims, preferred_element_type=F32)


def mm3(left, right, dims=AB):
    return mm(left[0], right[0], dims) + (mm(left[0], right[1], dims) + mm(left[1], right[0], dims))


def whiten(problems, b_ref, x_ref, g_ref):
    width = problems[0][0].shape[0]
    row = lax.broadcasted_iota(jnp.int32, (width, width), 0)
    col = lax.broadcasted_iota(jnp.int32, (width, width), 1)
    below, diag = row > col, row == col

    def half(value):
        return jnp.where(below, value, jnp.where(diag, 0.5 * value, 0.0))

    def factor(value):
        return jnp.where(below, -value, jnp.where(diag, 1.5 - 0.5 * value, 0.0)).astype(BF16)

    def advance(b, t, growth):
        b = mm(mm(t, b.astype(BF16)).astype(BF16), t, ABT) * growth
        return b, factor(b)

    def error(x, n):
        y_high, y_low = split(mm(x, g_ref[n, 0]) + mm(x, g_ref[n, 1]))
        return half(mm(y_high, x, ABT) + mm(y_low, x, ABT) - diag.astype(F32))

    rhs, worst, states = [], None, []
    for n, (gram, squares, cross) in enumerate(problems):
        ridge = squares / width + eps
        inv_root = lax.rsqrt(ridge)
        unit = gram * (inv_root * inv_root) + diag.astype(F32)
        g_ref[n, 0], g_ref[n, 1] = split(unit)
        rhs.append(split(cross * inv_root))
        high = unit.astype(BF16)
        square = mm(high, high)
        fourth = total(square * square)
        worst = fourth if worst is None else jnp.maximum(worst, fourth)
        scale = 1.9 * lax.rsqrt(jnp.sqrt(fourth))
        b = unit * scale
        t = factor(b)
        states.append((b, t, t.astype(F32) * jnp.sqrt(scale * (1.3 * 1.2))))
    worst = jnp.sum(worst)
    steps = jnp.int32(3)
    for bound in (16.0, 24.0, 45.0, 100.0, 180.0):
        steps = steps + (worst > bound**4).astype(jnp.int32)
    extra = (worst > 48.0**4).astype(jnp.int32)

    for growth in (1.3, 1.2):
        states = [(*advance(b, t, growth), x) for b, t, x in states]
        states = [(b, t, mm(t, x.astype(BF16))) for b, t, x in states]
    for n, (b, t, x) in enumerate(states):
        b_ref[n] = b
        x_ref[n] = x

    def more(_, carry):
        for n in range(len(problems)):
            b, t = advance(b_ref[n], factor(b_ref[n]), 1.0)
            b_ref[n], x_ref[n] = b, mm(t, x_ref[n].astype(BF16))
        return carry

    def fix(_, carry):
        for n in range(len(problems)):
            x = x_ref[n].astype(BF16)
            x_ref[n] = x.astype(F32) - mm(error(x, n).astype(BF16), x)
        return carry

    lax.fori_loop(3, steps, more, 0)
    lax.fori_loop(0, extra, fix, 0)
    outs = []
    for n in range(len(problems)):
        x = x_ref[n].astype(BF16)
        z = mm(x, rhs[n][0]) + mm(x, rhs[n][1])
        outs.append(z - mm(error(x, n).astype(BF16), z.astype(BF16)))
    return outs


def total(value):
    return jnp.sum(jnp.sum(value, axis=1, keepdims=True), axis=0, keepdims=True)


def leaf_kernel(rows_ref, out_ref, send_ref, *refs):
    s, u = rows_ref[0], rows_ref[1]
    wide = s.astype(F32)
    s_t = s.T
    (out,) = whiten([(mm(s_t, s), total(wide * wide), mm(s_t, u))], *refs)
    out_ref[...] = out
    send_ref[...] = out.astype(BF16)


def product(left, right):
    out = mm(left[0], right[0])
    if left[1] is not None:
        out += mm(left[1], right[0])
    if right[1] is not None:
        out += mm(left[0], right[1])
    return out


def merge_parts(p, q):
    p_t, q_t = (tuple(None if part is None else part.T for part in node) for node in (p, q))
    squares = 0.0
    for high, low in (p, q):
        wide = high.astype(F32) if low is None else high.astype(F32) + low.astype(F32)
        squares += total(wide * wide)
    return mm(p_t[0], p[0]) + mm(q_t[0], q[0]), squares, product(p_t, q) + product(q_t, p)


def merge_kernel(p_ref, q_ref, out_ref, *refs):
    near, far = whiten(
        [merge_parts((p_ref[...], None), (q_ref[0], None)), merge_parts((q_ref[1], None), (q_ref[2], None))], *refs
    )
    (out_ref[...],) = whiten([merge_parts(split(near), split(far))], *refs)


def dense_call(kernel, out_shapes, problems, *args):
    width = args[0].shape[-1]
    whole = pl.BlockSpec(memory_space=pltpu.VMEM)
    return pl.pallas_call(
        kernel,
        out_shape=tuple(jax.ShapeDtypeStruct((width, width), dtype) for dtype in out_shapes),
        in_specs=[whole] * len(args),
        out_specs=(whole,) * len(out_shapes),
        scratch_shapes=[
            pltpu.VMEM((problems, width, width), F32),
            pltpu.VMEM((problems, width, width), F32),
            pltpu.VMEM((problems, 2, width, width), BF16),
        ],
        compiler_params=pltpu.CompilerParams(vmem_limit_bytes=16 * 2**20),
    )(*args)


def gather_kernel(sent, out, send_sem, recv_sem):
    j = lax.axis_index("col")
    z = j % 4
    peers = [j - z + near for near in (z + 1 - 2 * (z % 2), (z + 2) % 4, 3 - z)]
    mesh_id = pl.DeviceIdType.MESH
    barrier = pltpu.get_barrier_semaphore()
    for peer in peers:
        pl.semaphore_signal(barrier, inc=1, device_id={"col": peer}, device_id_type=mesh_id)
    pl.semaphore_wait(barrier, 3)
    copies = [
        pltpu.make_async_remote_copy(
            src_ref=sent, dst_ref=out.at[n], send_sem=send_sem.at[n], recv_sem=recv_sem.at[n],
            device_id={"col": peer}, device_id_type=mesh_id,
        )
        for n, peer in enumerate(peers)
    ]
    for n in (1, 0, 2):
        copies[n].start()
    for copy in copies:
        copy.wait()


def gather_call(sent):
    anywhere = pl.BlockSpec(memory_space=pl.ANY)
    return pl.pallas_call(
        gather_kernel,
        out_shape=jax.ShapeDtypeStruct((3, *sent.shape), sent.dtype),
        in_specs=[anywhere],
        out_specs=anywhere,
        scratch_shapes=[pltpu.SemaphoreType.DMA((3,)), pltpu.SemaphoreType.DMA((3,))],
        compiler_params=pltpu.CompilerParams(collective_id=1, has_side_effects=True, vmem_limit_bytes=16 * 2**20),
    )(sent)


def iota(shape, axis):
    return lax.broadcasted_iota(jnp.int32, shape, axis)


def one_hot(condition):
    return jnp.where(condition, 1.0, 0.0).astype(BF16)


def column_of(row):
    n = row.shape[1]
    eye = one_hot(iota((n, n), 0) == iota((n, n), 1))
    return mm(eye, jnp.broadcast_to(row, (n, n)).astype(BF16), ABT)


def spread_matrix(leaf_row, tree_row, place_of_slot, slot_rank):
    n = leaf_row.shape[1]
    slots = place_of_slot.shape[0]
    here = leaf_row.astype(F32)
    twin = jnp.where((column_of(leaf_row) == here) & (iota((n, n), 0) < iota((n, n), 1)), 1.0, 0.0)
    rank = jnp.sum(twin, axis=0, keepdims=True)
    pick = one_hot(place_of_slot == iota((slots, n), 1))
    named = mm(pick, jnp.broadcast_to(tree_row, (n, n)).astype(BF16), ABT)
    return one_hot((named == here) & (slot_rank.astype(F32) == rank))


def sample_kernel(
    rows_n, cols_n, a_hbm, right_hbm, left_hbm, leaf_hbm, tree_hbm, out,
    leaf_ref, tree_ref, a_buf, right_buf, left_buf, left_t, fs, fr, bs, bp, bsum, br,
    f1s, f1r, f2s, b1s, b1r, b2s, acc,
    in_sem, fs_sem, fr_sem, ps_sem, pr_sem, bs_sem, br_sem,
    f1s_sem, f1r_sem, f2s_sem, f2r_sem, b1s_sem, b1r_sem, b2s_sem, b2r_sem,
):
    i, j = lax.axis_index("row"), lax.axis_index("col")
    lanes = fs.shape[1]
    group = cols_n // 4
    step_rows = group * lanes
    y0, z0 = j // group, j % group
    far_first = (2, 1, 3, 0)
    x0, core = i // 2, i % 2
    mesh_id = pl.DeviceIdType.MESH

    def remote(src, dst, send_sem, recv_sem, device):
        return pltpu.make_async_remote_copy(
            src_ref=src, dst_ref=dst, send_sem=send_sem, recv_sem=recv_sem, device_id=device, device_id_type=mesh_id
        )

    barrier = pltpu.get_barrier_semaphore()

    def greet_col(k, _):
        pl.semaphore_signal(barrier, inc=1, device_id={"col": (j + k) % cols_n}, device_id_type=mesh_id)
        return _

    def greet_row(k, _):
        pl.semaphore_signal(barrier, inc=1, device_id={"row": (i + k) % rows_n}, device_id_type=mesh_id)
        return _

    lax.fori_loop(1, cols_n, greet_col, 0)
    lax.fori_loop(1, rows_n, greet_row, 0)

    right_copy = pltpu.make_async_copy(right_hbm, right_buf, in_sem.at[4])
    leaf_copy = pltpu.make_async_copy(leaf_hbm, leaf_ref, in_sem.at[6])
    tree_copy = pltpu.make_async_copy(tree_hbm, tree_ref, in_sem.at[7])

    def rows_at(t):
        return pl.ds(pl.multiple_of(((y0 + far_first[t]) % 4) * step_rows, step_rows), step_rows)

    def a_copy(t):
        return pltpu.make_async_copy(a_hbm.at[rows_at(t)], a_buf.at[pl.ds(t * step_rows, step_rows)], in_sem.at[t])

    def left_copy(t):
        return pltpu.make_async_copy(
            left_hbm.at[rows_at(t)], left_buf.at[pl.ds(t * step_rows, step_rows)], in_sem.at[8 + t]
        )

    leaf_copy.start()
    tree_copy.start()
    a_copy(0).start()
    right_copy.start()
    for t in range(1, 4):
        a_copy(t).start()
    for t in range(4):
        left_copy(t).start()
    tiles = a_buf.shape[1] // lanes

    def mask(t):
        y = (y0 + far_first[t]) % 4
        for k in range(group):
            mine = column_of(leaf_ref[pl.ds(i * cols_n + y * group + k, 1), :]).astype(BF16)
            rows = slice(t * step_rows + k * lanes, t * step_rows + (k + 1) * lanes)
            for c in range(tiles):
                theirs = leaf_ref[pl.ds(j * rows_n + c, 1), :].astype(BF16)
                block = a_buf[rows, c * lanes : (c + 1) * lanes]
                a_buf[rows, c * lanes : (c + 1) * lanes] = jnp.where(mine == theirs, jnp.zeros_like(block), block)

    def forward(t):
        y = (y0 + far_first[t]) % 4
        part = mm(a_buf[t * step_rows : (t + 1) * step_rows, :], right_buf[...]).astype(BF16)
        fs[pl.ds(y * group, group)] = part.reshape(group, lanes, part.shape[1])

    def send(t):
        for dz in far_first:
            if (far_first[t], dz) != (0, 0):
                peer = ((y0 + far_first[t]) % 4) * group + (z0 + dz) % group
                remote(fs.at[peer], fr.at[j], fs_sem.at[peer], fr_sem.at[j], {"col": peer}).start()

    def turn(t):
        rows = slice(t * step_rows, (t + 1) * step_rows)
        left_t[:, rows] = left_buf[rows, :].T

    def distance(d):
        return min(d[0], 4 - d[0]) + min(d[1], 4 - d[1])

    near_first = sorted(((dy, dz) for dy in range(4) for dz in range(4) if (dy, dz) != (0, 0)), key=distance)

    leaf_copy.wait()
    tree_copy.wait()
    a_copy(0).wait()
    mask(0)
    right_copy.wait()
    a_copy(1).wait()
    mask(1)
    forward(0)
    pl.semaphore_wait(barrier, cols_n + rows_n - 2)
    send(0)
    a_copy(2).wait()
    left_copy(0).wait()
    left_copy(1).wait()
    mask(2)
    forward(1)
    send(1)
    turn(0)
    turn(1)
    a_copy(3).wait()
    left_copy(2).wait()
    left_copy(3).wait()
    mask(3)
    forward(2)
    send(2)
    turn(2)
    turn(3)
    forward(3)
    send(3)

    other = 1 - core
    chips = rows_n // 2

    def pair(x):
        return remote(bs.at[other, x], bp.at[x], ps_sem.at[x], pr_sem.at[x], {"row": x0 * 2 + other})

    def along(x):
        return remote(bsum.at[x], br.at[x0], bs_sem.at[x], br_sem.at[x0], {"row": x * 2 + core})

    for dx in far_first:
        x = (x0 + dx) % chips
        part = mm(left_t[...], a_buf[:, pl.ds(pl.multiple_of(x * 2 * lanes, 2 * lanes), 2 * lanes)])
        bs[0, pl.ds(x, 1)] = part[None, :, :lanes]
        bs[1, pl.ds(x, 1)] = part[None, :, lanes:]
        pair(x).start()
    for dx in far_first:
        x = (x0 + dx) % chips
        pair(x).wait()
        bsum[pl.ds(x, 1)] = bs[core, pl.ds(x, 1)] + bp[pl.ds(x, 1)]
        if dx:
            along(x).start()

    tree = tree_ref[...]
    slots = out.shape[1]
    slot = iota((slots, lanes), 0)
    row_bits, col_bits = rows_n.bit_length() - 1, cols_n.bit_length() - 1
    f_place = (((slot >> 1) & (rows_n - 1)) << col_bits) + (slot >> (1 + row_bits))
    forward_map = spread_matrix(leaf_ref[pl.ds(i * cols_n + j, 1), :], tree, f_place, slot & 1)
    backward_map = spread_matrix(leaf_ref[pl.ds(j * rows_n + i, 1), :], tree, slot >> 1, slot & 1)

    def along_end(k, carry):
        x = (x0 + 1 + k) % chips
        along(x).wait_send()
        remote(bsum.at[x], br.at[x], bs_sem.at[x], br_sem.at[x], {"row": x * 2 + core}).wait_recv()
        return carry

    lax.fori_loop(0, chips - 1, along_end, 0)
    br[pl.ds(x0, 1)] = bsum[pl.ds(x0, 1)]
    sample_back = jnp.sum(br[...], axis=0).astype(BF16)
    width = out.shape[2]

    def rows_exchange(src, dst, send_sem, recv_sem):
        def start(k, carry):
            peer = (i + k) % rows_n
            remote(src.at[peer], dst.at[i], send_sem.at[peer], recv_sem.at[i], {"row": peer}).start()
            return carry

        def end(k, carry):
            peer = (i + k) % rows_n
            remote(src.at[peer], dst.at[peer], send_sem.at[peer], recv_sem.at[peer], {"row": peer}).wait()
            return carry

        return start, end

    def cols_exchange(src, dst, send_sem, recv_sem):
        def start(k, carry):
            peer = (j + k) % cols_n
            remote(src.at[peer], dst.at[j], send_sem.at[peer], recv_sem.at[j], {"col": peer}).start()
            return carry

        def end(k, carry):
            peer = (j + k) % cols_n
            remote(src.at[peer], dst.at[peer], send_sem.at[peer], recv_sem.at[peer], {"col": peer}).wait()
            return carry

        return start, end

    b1_start, b1_end = rows_exchange(b1s, b1r, b1s_sem, b1r_sem)
    f1_end = cols_exchange(f1s, f1r, f1s_sem, f1r_sem)[1]

    def back_part(col):
        return out.at[1, pl.ds(pl.multiple_of(col * 2 * rows_n, 2 * rows_n), 2 * rows_n)]

    def forward_part(row):
        return out.at[0, pl.ds(pl.multiple_of(row * 2 * cols_n, 2 * cols_n), 2 * cols_n)]

    def b2_end(k, carry):
        peer = (j + k) % cols_n
        remote(b2s.at[peer], back_part(peer), b2s_sem.at[peer], b2r_sem.at[peer], {"col": peer}).wait()
        return carry

    def f2_start(k, carry):
        peer = (i + k) % rows_n
        remote(f2s.at[peer], forward_part(i), f2s_sem.at[peer], f2r_sem.at[i], {"row": peer}).start()
        return carry

    def f2_end(k, carry):
        peer = (i + k) % rows_n
        remote(f2s.at[peer], forward_part(peer), f2s_sem.at[peer], f2r_sem.at[peer], {"row": peer}).wait()
        return carry

    b1s[...] = mm(backward_map, sample_back, ABT).astype(BF16).reshape(b1s.shape)
    lax.fori_loop(1, rows_n, b1_start, 0)
    b1r[pl.ds(i, 1)] = b1s[pl.ds(i, 1)]

    acc[...] = fs[pl.ds(j, 1)][0].astype(F32)
    for dy, dz in near_first:
        peer = ((y0 + dy) % 4) * group + (z0 + dz) % group
        remote(fs.at[peer], fr.at[peer], fs_sem.at[peer], fr_sem.at[peer], {"col": peer}).wait()
        acc[...] += fr[pl.ds(peer, 1)][0].astype(F32)
    f1s[...] = mm(forward_map, acc[...].astype(BF16)).astype(BF16).reshape(f1s.shape)
    for dy, dz in reversed(near_first):
        peer = ((y0 + dy) % 4) * group + (z0 + dz) % group
        remote(f1s.at[peer], f1r.at[j], f1s_sem.at[peer], f1r_sem.at[j], {"col": peer}).start()
    f1r[pl.ds(j, 1)] = f1s[pl.ds(j, 1)]

    slot = iota((slots, slots), 0)
    source = iota((slots, slots), 1)
    row_col = (((slot >> 1) & (cols_n - 1)) << (1 + row_bits)) + ((slot >> (1 + col_bits)) << 1) + (slot & 1)
    col_row = (((slot >> 1) & (rows_n - 1)) << (1 + col_bits)) + ((slot >> (1 + row_bits)) << 1) + (slot & 1)
    to_rows, to_cols = one_hot(source == row_col), one_hot(source == col_row)

    lax.fori_loop(1, rows_n, b1_end, 0)
    b2s[...] = mm(to_cols, b1r[...].reshape(slots, width)).astype(BF16).reshape(b2s.shape)
    for dy, dz in reversed(near_first):
        peer = ((y0 + dy) % 4) * group + (z0 + dz) % group
        remote(b2s.at[peer], back_part(j), b2s_sem.at[peer], b2r_sem.at[j], {"col": peer}).start()
    back_own = pltpu.make_async_copy(b2s.at[j], back_part(j), in_sem.at[4])
    back_own.start()

    lax.fori_loop(1, cols_n, f1_end, 0)
    f2s[...] = mm(to_rows, f1r[...].reshape(slots, width)).astype(BF16).reshape(f2s.shape)
    lax.fori_loop(1, rows_n, f2_start, 0)
    forward_own = pltpu.make_async_copy(f2s.at[i], forward_part(i), in_sem.at[5])
    forward_own.start()

    back_own.wait()
    forward_own.wait()
    lax.fori_loop(1, cols_n, b2_end, 0)
    lax.fori_loop(1, rows_n, f2_end, 0)


def sample_call(front_block, probe_right, probe_left, leaves, tree, rows_n, cols_n):
    tile_rows, tile_cols = front_block.shape
    samples = probe_right.shape[1]
    lanes = leaves.shape[1]
    slots = 2 * rows_n * cols_n
    chips = rows_n // 2
    hbm = pl.BlockSpec(memory_space=pltpu.HBM)
    out = jax.ShapeDtypeStruct((2, slots, samples), BF16)
    by_col = pltpu.VMEM((cols_n, 2 * rows_n, samples), BF16)
    by_row = pltpu.VMEM((rows_n, 2 * cols_n, samples), BF16)
    dma = pltpu.SemaphoreType.DMA
    return pl.pallas_call(
        functools.partial(sample_kernel, rows_n, cols_n),
        out_shape=out,
        in_specs=[hbm] * 5,
        out_specs=pl.BlockSpec(memory_space=pl.ANY),
        scratch_shapes=[
            pltpu.VMEM(leaves.shape, jnp.int32),
            pltpu.VMEM(tree.shape, jnp.int32),
            pltpu.VMEM((tile_rows, tile_cols), BF16),
            pltpu.VMEM((tile_cols, samples), BF16),
            pltpu.VMEM((tile_rows, samples), BF16),
            pltpu.VMEM((samples, tile_rows), BF16),
            pltpu.VMEM((cols_n, lanes, samples), BF16),
            pltpu.VMEM((cols_n, lanes, samples), BF16),
            pltpu.VMEM((2, chips, samples, lanes), F32),
            pltpu.VMEM((chips, samples, lanes), F32),
            pltpu.VMEM((chips, samples, lanes), F32),
            pltpu.VMEM((chips, samples, lanes), F32),
            by_col, by_col, by_row, by_row, by_row, by_col,
            pltpu.VMEM((lanes, samples), F32),
            dma((12,)),
            dma((cols_n,)), dma((cols_n,)),
            dma((chips,)), dma((chips,)), dma((chips,)), dma((chips,)),
            dma((cols_n,)), dma((cols_n,)), dma((rows_n,)), dma((rows_n,)),
            dma((rows_n,)), dma((rows_n,)), dma((cols_n,)), dma((cols_n,)),
        ],
        compiler_params=pltpu.CompilerParams(collective_id=0, has_side_effects=True, vmem_limit_bytes=67043328),
    )(front_block, probe_right, probe_left, leaves, tree)


def per_device(front_block, probe_right, probe_left, row_leaf, tree_leaf):
    rows_n, cols_n = lax.axis_size("row"), lax.axis_size("col")
    devices = rows_n * cols_n
    leaves = row_leaf.reshape(devices, row_leaf.shape[0] // devices)
    routed = sample_call(front_block, probe_right, probe_left, leaves, tree_leaf.reshape(1, devices), rows_n, cols_n)
    coupling, sent = dense_call(leaf_kernel, (F32, BF16), 1, routed)
    (merged,) = dense_call(merge_kernel, (F32,), 2, sent, gather_call(sent))
    return (coupling[None], merged[None])


def solution(mesh):
    return jax.shard_map(
        per_device,
        mesh=mesh,
        in_specs=(P("row", "col"), P("col", None), P("row", None), P(), P()),
        out_specs=(P(("row", "col"), None, None), P(("row", "col"), None, None)),
        check_vma=False,
    )
```

```python
import functools

import jax
import jax.numpy as jnp
from jax import lax
from jax.experimental import pallas as pl
from jax.experimental.pallas import tpu as pltpu
from jax.sharding import PartitionSpec as P

eps = 1e-05
F32, BF16 = jnp.float32, jnp.bfloat16
AB = (((1,), (0,)), ((), ()))
ABT = (((1,), (1,)), ((), ()))
ATB = (((0,), (0,)), ((), ()))


def split(value):
    high = value.astype(BF16)
    return high, (value - high.astype(F32)).astype(BF16)


def mm(left, right, dims=AB):
    return lax.dot_general(left, right, dims, preferred_element_type=F32)


def mm3(left, right, dims=AB):
    return mm(left[0], right[0], dims) + (mm(left[0], right[1], dims) + mm(left[1], right[0], dims))


def whiten(problems, b_ref, x_ref, g_ref):
    width = problems[0][0].shape[0]
    row = lax.broadcasted_iota(jnp.int32, (width, width), 0)
    col = lax.broadcasted_iota(jnp.int32, (width, width), 1)
    below, diag = row > col, row == col

    def half(value):
        return jnp.where(below, value, jnp.where(diag, 0.5 * value, 0.0))

    def factor(value):
        return jnp.where(below, -value, jnp.where(diag, 1.5 - 0.5 * value, 0.0)).astype(BF16)

    def advance(b, t, growth):
        b = mm(mm(t, b.astype(BF16)).astype(BF16), t, ABT) * growth
        return b, factor(b)

    def error(x, n):
        y_high, y_low = split(mm(x, g_ref[n, 0]) + mm(x, g_ref[n, 1]))
        return half(mm(y_high, x, ABT) + mm(y_low, x, ABT) - diag.astype(F32))

    rhs, worst, states = [], None, []
    for n, (gram, squares, cross) in enumerate(problems):
        ridge = squares / width + eps
        inv_root = lax.rsqrt(ridge)
        unit = gram * (inv_root * inv_root) + diag.astype(F32)
        g_ref[n, 0], g_ref[n, 1] = split(unit)
        rhs.append(split(cross * inv_root))
        high = unit.astype(BF16)
        square = mm(high, high)
        fourth = total(square * square)
        worst = fourth if worst is None else jnp.maximum(worst, fourth)
        scale = 1.9 * lax.rsqrt(jnp.sqrt(fourth))
        b = unit * scale
        t = factor(b)
        states.append((b, t, t.astype(F32) * jnp.sqrt(scale * (1.3 * 1.2))))
    worst = jnp.sum(worst)
    steps = jnp.int32(3)
    for bound in (16.0, 24.0, 45.0, 100.0, 180.0):
        steps = steps + (worst > bound**4).astype(jnp.int32)
    extra = (worst > 48.0**4).astype(jnp.int32)

    for growth in (1.3, 1.2):
        states = [(*advance(b, t, growth), x) for b, t, x in states]
        states = [(b, t, mm(t, x.astype(BF16))) for b, t, x in states]
    for n, (b, t, x) in enumerate(states):
        b_ref[n] = b
        x_ref[n] = x

    def more(_, carry):
        for n in range(len(problems)):
            b, t = advance(b_ref[n], factor(b_ref[n]), 1.0)
            b_ref[n], x_ref[n] = b, mm(t, x_ref[n].astype(BF16))
        return carry

    def fix(_, carry):
        for n in range(len(problems)):
            x = x_ref[n].astype(BF16)
            x_ref[n] = x.astype(F32) - mm(error(x, n).astype(BF16), x)
        return carry

    lax.fori_loop(3, steps, more, 0)
    lax.fori_loop(0, extra, fix, 0)
    outs = []
    for n in range(len(problems)):
        x = x_ref[n].astype(BF16)
        z = mm(x, rhs[n][0]) + mm(x, rhs[n][1])
        outs.append(z - mm(error(x, n).astype(BF16), z.astype(BF16)))
    return outs


def total(value):
    return jnp.sum(jnp.sum(value, axis=1, keepdims=True), axis=0, keepdims=True)


def leaf_kernel(rows_ref, out_ref, send_ref, *refs):
    s, u = rows_ref[0], rows_ref[1]
    wide = s.astype(F32)
    s_t = s.T
    (out,) = whiten([(mm(s_t, s), total(wide * wide), mm(s_t, u))], *refs)
    out_ref[...] = out
    send_ref[...] = out.astype(BF16)


def product(left, right):
    out = mm(left[0], right[0])
    if left[1] is not None:
        out += mm(left[1], right[0])
    if right[1] is not None:
        out += mm(left[0], right[1])
    return out


def merge_parts(p, q):
    p_t, q_t = (tuple(None if part is None else part.T for part in node) for node in (p, q))
    squares = 0.0
    for high, low in (p, q):
        wide = high.astype(F32) if low is None else high.astype(F32) + low.astype(F32)
        squares += total(wide * wide)
    return mm(p_t[0], p[0]) + mm(q_t[0], q[0]), squares, product(p_t, q) + product(q_t, p)


def merge_kernel(p_ref, q_ref, out_ref, *refs):
    near, far = whiten(
        [merge_parts((p_ref[...], None), (q_ref[0], None)), merge_parts((q_ref[1], None), (q_ref[2], None))], *refs
    )
    (out_ref[...],) = whiten([merge_parts(split(near), split(far))], *refs)


def dense_call(kernel, out_shapes, problems, *args):
    width = args[0].shape[-1]
    whole = pl.BlockSpec(memory_space=pltpu.VMEM)
    return pl.pallas_call(
        kernel,
        out_shape=tuple(jax.ShapeDtypeStruct((width, width), dtype) for dtype in out_shapes),
        in_specs=[whole] * len(args),
        out_specs=(whole,) * len(out_shapes),
        scratch_shapes=[
            pltpu.VMEM((problems, width, width), F32),
            pltpu.VMEM((problems, width, width), F32),
            pltpu.VMEM((problems, 2, width, width), BF16),
        ],
        compiler_params=pltpu.CompilerParams(vmem_limit_bytes=16 * 2**20),
    )(*args)


def gather_kernel(sent, out, send_sem, recv_sem):
    j = lax.axis_index("col")
    z = j % 4
    peers = [j - z + near for near in (z + 1 - 2 * (z % 2), (z + 2) % 4, 3 - z)]
    mesh_id = pl.DeviceIdType.MESH
    barrier = pltpu.get_barrier_semaphore()
    for peer in peers:
        pl.semaphore_signal(barrier, inc=1, device_id={"col": peer}, device_id_type=mesh_id)
    pl.semaphore_wait(barrier, 3)
    copies = [
        pltpu.make_async_remote_copy(
            src_ref=sent, dst_ref=out.at[n], send_sem=send_sem.at[n], recv_sem=recv_sem.at[n],
            device_id={"col": peer}, device_id_type=mesh_id,
        )
        for n, peer in enumerate(peers)
    ]
    for n in (1, 0, 2):
        copies[n].start()
    for copy in copies:
        copy.wait()


def gather_call(sent):
    anywhere = pl.BlockSpec(memory_space=pl.ANY)
    return pl.pallas_call(
        gather_kernel,
        out_shape=jax.ShapeDtypeStruct((3, *sent.shape), sent.dtype),
        in_specs=[anywhere],
        out_specs=anywhere,
        scratch_shapes=[pltpu.SemaphoreType.DMA((3,)), pltpu.SemaphoreType.DMA((3,))],
        compiler_params=pltpu.CompilerParams(collective_id=1, has_side_effects=True, vmem_limit_bytes=16 * 2**20),
    )(sent)


def iota(shape, axis):
    return lax.broadcasted_iota(jnp.int32, shape, axis)


def one_hot(condition):
    return jnp.where(condition, 1.0, 0.0).astype(BF16)


def column_of(row):
    n = row.shape[1]
    eye = one_hot(iota((n, n), 0) == iota((n, n), 1))
    return mm(eye, jnp.broadcast_to(row, (n, n)).astype(BF16), ABT)


def spread_matrix(leaf_row, tree_row, place_of_slot, slot_rank):
    n = leaf_row.shape[1]
    slots = place_of_slot.shape[0]
    here = leaf_row.astype(F32)
    twin = jnp.where((column_of(leaf_row) == here) & (iota((n, n), 0) < iota((n, n), 1)), 1.0, 0.0)
    rank = jnp.sum(twin, axis=0, keepdims=True)
    pick = one_hot(place_of_slot == iota((slots, n), 1))
    named = mm(pick, jnp.broadcast_to(tree_row, (n, n)).astype(BF16), ABT)
    return one_hot((named == here) & (slot_rank.astype(F32) == rank))


def sample_kernel(
    rows_n, cols_n, a_hbm, right_hbm, left_hbm, leaf_hbm, tree_hbm, out,
    leaf_ref, tree_ref, a_buf, right_buf, left_buf, left_t, fs, fr, bs, bp, bsum, br,
    f1s, f1r, f2s, b1s, b1r, b2s, acc,
    in_sem, fs_sem, fr_sem, ps_sem, pr_sem, bs_sem, br_sem,
    f1s_sem, f1r_sem, f2s_sem, f2r_sem, b1s_sem, b1r_sem, b2s_sem, b2r_sem,
):
    i, j = lax.axis_index("row"), lax.axis_index("col")
    lanes = fs.shape[1]
    group = cols_n // 4
    step_rows = group * lanes
    y0, z0 = j // group, j % group
    far_first = (2, 1, 3, 0)
    x0, core = i // 2, i % 2
    mesh_id = pl.DeviceIdType.MESH

    def remote(src, dst, send_sem, recv_sem, device):
        return pltpu.make_async_remote_copy(
            src_ref=src, dst_ref=dst, send_sem=send_sem, recv_sem=recv_sem, device_id=device, device_id_type=mesh_id
        )

    barrier = pltpu.get_barrier_semaphore()

    def distance(d):
        return min(d[0], 4 - d[0]) + min(d[1], 4 - d[1])

    near_first = sorted(((dy, dz) for dy in range(4) for dz in range(4) if (dy, dz) != (0, 0)), key=distance)

    for dy, dz in reversed(near_first):
        peer = ((y0 + dy) % 4) * group + (z0 + dz) % group
        pl.semaphore_signal(barrier, inc=1, device_id={"col": peer}, device_id_type=mesh_id)
    rows_far_first = (4, 5, 3, 2, 6, 7, 1)
    for k in rows_far_first:
        pl.semaphore_signal(barrier, inc=1, device_id={"row": (i + k) % rows_n}, device_id_type=mesh_id)

    right_copy = pltpu.make_async_copy(right_hbm, right_buf, in_sem.at[4])
    leaf_copy = pltpu.make_async_copy(leaf_hbm, leaf_ref, in_sem.at[6])
    tree_copy = pltpu.make_async_copy(tree_hbm, tree_ref, in_sem.at[7])

    def rows_at(t):
        return pl.ds(pl.multiple_of(((y0 + far_first[t]) % 4) * step_rows, step_rows), step_rows)

    def a_copy(t):
        return pltpu.make_async_copy(a_hbm.at[rows_at(t)], a_buf.at[pl.ds(t * step_rows, step_rows)], in_sem.at[t])

    def left_copy(t):
        return pltpu.make_async_copy(
            left_hbm.at[rows_at(t)], left_buf.at[pl.ds(t * step_rows, step_rows)], in_sem.at[8 + t]
        )

    leaf_copy.start()
    tree_copy.start()
    a_copy(0).start()
    right_copy.start()
    for t in range(1, 4):
        a_copy(t).start()
    for t in range(4):
        left_copy(t).start()
    tiles = a_buf.shape[1] // lanes

    def mask(t):
        y = (y0 + far_first[t]) % 4
        for k in range(group):
            mine = column_of(leaf_ref[pl.ds(i * cols_n + y * group + k, 1), :]).astype(BF16)
            rows = slice(t * step_rows + k * lanes, t * step_rows + (k + 1) * lanes)
            for c in range(tiles):
                theirs = leaf_ref[pl.ds(j * rows_n + c, 1), :].astype(BF16)
                block = a_buf[rows, c * lanes : (c + 1) * lanes]
                a_buf[rows, c * lanes : (c + 1) * lanes] = jnp.where(mine == theirs, jnp.zeros_like(block), block)

    def forward(t):
        y = (y0 + far_first[t]) % 4
        part = mm(a_buf[t * step_rows : (t + 1) * step_rows, :], right_buf[...]).astype(BF16)
        fs[pl.ds(y * group, group)] = part.reshape(group, lanes, part.shape[1])

    def send(t):
        for dz in far_first:
            if (far_first[t], dz) != (0, 0):
                peer = ((y0 + far_first[t]) % 4) * group + (z0 + dz) % group
                remote(fs.at[peer], fr.at[j], fs_sem.at[peer], fr_sem.at[j], {"col": peer}).start()

    def turn(t):
        rows = slice(t * step_rows, (t + 1) * step_rows)
        left_t[:, rows] = left_buf[rows, :].T

    leaf_copy.wait()
    tree_copy.wait()
    a_copy(0).wait()
    mask(0)
    right_copy.wait()
    a_copy(1).wait()
    mask(1)
    forward(0)
    pl.semaphore_wait(barrier, cols_n + rows_n - 2)
    send(0)
    a_copy(2).wait()
    left_copy(0).wait()
    left_copy(1).wait()
    mask(2)
    forward(1)
    send(1)
    turn(0)
    turn(1)
    a_copy(3).wait()
    left_copy(2).wait()
    left_copy(3).wait()
    mask(3)
    forward(2)
    send(2)
    turn(2)
    turn(3)
    forward(3)
    send(3)

    other = 1 - core
    chips = rows_n // 2

    def pair(x):
        return remote(bs.at[other, x], bp.at[x], ps_sem.at[x], pr_sem.at[x], {"row": x0 * 2 + other})

    def along(x):
        return remote(bsum.at[x], br.at[x0], bs_sem.at[x], br_sem.at[x0], {"row": x * 2 + core})

    for dx in far_first:
        x = (x0 + dx) % chips
        part = mm(left_t[...], a_buf[:, pl.ds(pl.multiple_of(x * 2 * lanes, 2 * lanes), 2 * lanes)])
        bs[0, pl.ds(x, 1)] = part[None, :, :lanes]
        bs[1, pl.ds(x, 1)] = part[None, :, lanes:]
        pair(x).start()
    for dx in far_first:
        x = (x0 + dx) % chips
        pair(x).wait()
        bsum[pl.ds(x, 1)] = bs[core, pl.ds(x, 1)] + bp[pl.ds(x, 1)]
        if dx:
            along(x).start()

    tree = tree_ref[...]
    slots = out.shape[1]
    slot = iota((slots, lanes), 0)
    row_bits, col_bits = rows_n.bit_length() - 1, cols_n.bit_length() - 1
    f_place = (((slot >> 1) & (rows_n - 1)) << col_bits) + (slot >> (1 + row_bits))
    forward_map = spread_matrix(leaf_ref[pl.ds(i * cols_n + j, 1), :], tree, f_place, slot & 1)
    backward_map = spread_matrix(leaf_ref[pl.ds(j * rows_n + i, 1), :], tree, slot >> 1, slot & 1)

    def along_end(k, carry):
        x = (x0 + 1 + k) % chips
        along(x).wait_send()
        remote(bsum.at[x], br.at[x], bs_sem.at[x], br_sem.at[x], {"row": x * 2 + core}).wait_recv()
        return carry

    lax.fori_loop(0, chips - 1, along_end, 0)
    br[pl.ds(x0, 1)] = bsum[pl.ds(x0, 1)]
    sample_back = jnp.sum(br[...], axis=0).astype(BF16)
    width = out.shape[2]

    def rows_exchange(src, dst, send_sem, recv_sem):
        def start(k, carry):
            peer = (i + k) % rows_n
            remote(src.at[peer], dst.at[i], send_sem.at[peer], recv_sem.at[i], {"row": peer}).start()
            return carry

        def end(k, carry):
            peer = (i + k) % rows_n
            remote(src.at[peer], dst.at[peer], send_sem.at[peer], recv_sem.at[peer], {"row": peer}).wait()
            return carry

        return start, end

    def cols_exchange(src, dst, send_sem, recv_sem):
        def start(k, carry):
            peer = (j + k) % cols_n
            remote(src.at[peer], dst.at[j], send_sem.at[peer], recv_sem.at[j], {"col": peer}).start()
            return carry

        def end(k, carry):
            peer = (j + k) % cols_n
            remote(src.at[peer], dst.at[peer], send_sem.at[peer], recv_sem.at[peer], {"col": peer}).wait()
            return carry

        return start, end

    b1_start, b1_end = rows_exchange(b1s, b1r, b1s_sem, b1r_sem)
    f1_end = cols_exchange(f1s, f1r, f1s_sem, f1r_sem)[1]

    def back_part(col):
        return out.at[1, pl.ds(pl.multiple_of(col * 2 * rows_n, 2 * rows_n), 2 * rows_n)]

    def forward_part(row):
        return out.at[0, pl.ds(pl.multiple_of(row * 2 * cols_n, 2 * cols_n), 2 * cols_n)]

    def b2_end(k, carry):
        peer = (j + k) % cols_n
        remote(b2s.at[peer], back_part(peer), b2s_sem.at[peer], b2r_sem.at[peer], {"col": peer}).wait()
        return carry

    def f2_start(k, carry):
        peer = (i + k) % rows_n
        remote(f2s.at[peer], forward_part(i), f2s_sem.at[peer], f2r_sem.at[i], {"row": peer}).start()
        return carry

    def f2_end(k, carry):
        peer = (i + k) % rows_n
        remote(f2s.at[peer], forward_part(peer), f2s_sem.at[peer], f2r_sem.at[peer], {"row": peer}).wait()
        return carry

    b1s[...] = mm(backward_map, sample_back, ABT).astype(BF16).reshape(b1s.shape)
    lax.fori_loop(1, rows_n, b1_start, 0)
    b1r[pl.ds(i, 1)] = b1s[pl.ds(i, 1)]

    acc[...] = fs[pl.ds(j, 1)][0].astype(F32)
    for dy, dz in near_first:
        peer = ((y0 + dy) % 4) * group + (z0 + dz) % group
        remote(fs.at[peer], fr.at[peer], fs_sem.at[peer], fr_sem.at[peer], {"col": peer}).wait()
        acc[...] += fr[pl.ds(peer, 1)][0].astype(F32)
    f1s[...] = mm(forward_map, acc[...].astype(BF16)).astype(BF16).reshape(f1s.shape)
    for dy, dz in reversed(near_first):
        peer = ((y0 + dy) % 4) * group + (z0 + dz) % group
        remote(f1s.at[peer], f1r.at[j], f1s_sem.at[peer], f1r_sem.at[j], {"col": peer}).start()
    f1r[pl.ds(j, 1)] = f1s[pl.ds(j, 1)]

    slot = iota((slots, slots), 0)
    source = iota((slots, slots), 1)
    row_col = (((slot >> 1) & (cols_n - 1)) << (1 + row_bits)) + ((slot >> (1 + col_bits)) << 1) + (slot & 1)
    col_row = (((slot >> 1) & (rows_n - 1)) << (1 + col_bits)) + ((slot >> (1 + row_bits)) << 1) + (slot & 1)
    to_rows, to_cols = one_hot(source == row_col), one_hot(source == col_row)

    lax.fori_loop(1, rows_n, b1_end, 0)
    b2s[...] = mm(to_cols, b1r[...].reshape(slots, width)).astype(BF16).reshape(b2s.shape)
    for dy, dz in reversed(near_first):
        peer = ((y0 + dy) % 4) * group + (z0 + dz) % group
        remote(b2s.at[peer], back_part(j), b2s_sem.at[peer], b2r_sem.at[j], {"col": peer}).start()
    back_own = pltpu.make_async_copy(b2s.at[j], back_part(j), in_sem.at[4])
    back_own.start()

    lax.fori_loop(1, cols_n, f1_end, 0)
    f2s[...] = mm(to_rows, f1r[...].reshape(slots, width)).astype(BF16).reshape(f2s.shape)
    for k in rows_far_first:
        f2_start(k, 0)
    forward_own = pltpu.make_async_copy(f2s.at[i], forward_part(i), in_sem.at[5])
    forward_own.start()

    back_own.wait()
    forward_own.wait()
    lax.fori_loop(1, cols_n, b2_end, 0)
    lax.fori_loop(1, rows_n, f2_end, 0)


def sample_call(front_block, probe_right, probe_left, leaves, tree, rows_n, cols_n):
    tile_rows, tile_cols = front_block.shape
    samples = probe_right.shape[1]
    lanes = leaves.shape[1]
    slots = 2 * rows_n * cols_n
    chips = rows_n // 2
    hbm = pl.BlockSpec(memory_space=pltpu.HBM)
    out = jax.ShapeDtypeStruct((2, slots, samples), BF16)
    by_col = pltpu.VMEM((cols_n, 2 * rows_n, samples), BF16)
    by_row = pltpu.VMEM((rows_n, 2 * cols_n, samples), BF16)
    dma = pltpu.SemaphoreType.DMA
    return pl.pallas_call(
        functools.partial(sample_kernel, rows_n, cols_n),
        out_shape=out,
        in_specs=[hbm] * 5,
        out_specs=pl.BlockSpec(memory_space=pl.ANY),
        scratch_shapes=[
            pltpu.VMEM(leaves.shape, jnp.int32),
            pltpu.VMEM(tree.shape, jnp.int32),
            pltpu.VMEM((tile_rows, tile_cols), BF16),
            pltpu.VMEM((tile_cols, samples), BF16),
            pltpu.VMEM((tile_rows, samples), BF16),
            pltpu.VMEM((samples, tile_rows), BF16),
            pltpu.VMEM((cols_n, lanes, samples), BF16),
            pltpu.VMEM((cols_n, lanes, samples), BF16),
            pltpu.VMEM((2, chips, samples, lanes), F32),
            pltpu.VMEM((chips, samples, lanes), F32),
            pltpu.VMEM((chips, samples, lanes), F32),
            pltpu.VMEM((chips, samples, lanes), F32),
            by_col, by_col, by_row, by_row, by_row, by_col,
            pltpu.VMEM((lanes, samples), F32),
            dma((12,)),
            dma((cols_n,)), dma((cols_n,)),
            dma((chips,)), dma((chips,)), dma((chips,)), dma((chips,)),
            dma((cols_n,)), dma((cols_n,)), dma((rows_n,)), dma((rows_n,)),
            dma((rows_n,)), dma((rows_n,)), dma((cols_n,)), dma((cols_n,)),
        ],
        compiler_params=pltpu.CompilerParams(collective_id=0, has_side_effects=True, vmem_limit_bytes=67043328),
    )(front_block, probe_right, probe_left, leaves, tree)


def per_device(front_block, probe_right, probe_left, row_leaf, tree_leaf):
    rows_n, cols_n = lax.axis_size("row"), lax.axis_size("col")
    devices = rows_n * cols_n
    leaves = row_leaf.reshape(devices, row_leaf.shape[0] // devices)
    routed = sample_call(front_block, probe_right, probe_left, leaves, tree_leaf.reshape(1, devices), rows_n, cols_n)
    coupling, sent = dense_call(leaf_kernel, (F32, BF16), 1, routed)
    (merged,) = dense_call(merge_kernel, (F32,), 2, sent, gather_call(sent))
    return (coupling[None], merged[None])


def solution(mesh):
    return jax.shard_map(
        per_device,
        mesh=mesh,
        in_specs=(P("row", "col"), P("col", None), P("row", None), P(), P()),
        out_specs=(P(("row", "col"), None, None), P(("row", "col"), None, None)),
        check_vma=False,
    )
```
